512 devices in a mesh: strike: 64 (over y_hi, z, x), normal: 8 (over y_lo, core).
Axes of the slice: x: 4, y: 8 (y_hi: 2, y_lo: 4; y = y_hi * 4 + y_lo), z: 8, core: 2. Of those that a mesh axis runs over, the one named last changes fastest.
Arguments:
- displacement: float32 [3, 2048, 64, 128], P(None, 'strike', 'normal'), may hold values from -6 to 6
- velocity: float32 [3, 2048, 64, 128], P(None, 'strike', 'normal'), may hold values from -6 to 6
- stiffness: float32 [2048, 64, 128], P('strike', 'normal'), may hold values from 0.4 to 1.3
- yield_flags: int32 [512, 64, 32], P('strike', 'normal'), may hold values from 0 to 1
- contact: int32 [2, 2048, 128], P(None, 'strike'), may hold values 0 or 1
- history: bfloat16 [2, 8, 2, 3, 128, 2048], P(None, None, None, None, 'strike'), may hold values from -6 to 6
- kernel: float32 [2, 8, 3, 2048], replicated, may hold values from -1.8 to 1.8
Outputs:
- final_displacement: float32 [3, 2048, 64, 128], P(None, 'strike', 'normal')
- final_velocity: float32 [3, 2048, 64, 128], P(None, 'strike', 'normal')
The draws below stay inside these ranges and needn't reach their ends.
All inputs are finite; a program needn't handle non-finite values. No bound on the sum of `contact` on one device may be relied on, other than what follows from the above.
Results may differ from the reference program's by a relative error of at most 0.001.
Values may be sent and summed in bfloat16 or wider, within the bound.
A program may use at most 64 MiB of HBM per device.

```python
import math
import jax
import jax.numpy as jnp
from jax import lax

ND = 128
HIST = 8
SUB = 3
BLK = 4
NS = 2048
NN = 64


def plant(entries, rng, low, largest):
    place = [jax.random.randint(jax.random.fold_in(rng, axis), (), 0, length) for axis, length in enumerate(entries.shape)]
    main_axis = entries.shape.index(max(entries.shape))
    neighbour = place[:main_axis] + [(place[main_axis] + 1) % entries.shape[main_axis]] + place[main_axis + 1:]
    return entries.at[tuple(place)].set(low).at[tuple(neighbour)].set(largest)


def levels(key, extent, pieces, least, largest):
    gain = 1.0
    for dim, parts in pieces:
        draws = jax.random.uniform(jax.random.fold_in(jax.random.fold_in(key, 6), dim), (parts,), jnp.float32, least / len(pieces), largest / len(pieces))
        gain = gain * jnp.repeat(jnp.exp(draws), extent[dim] // parts).reshape((-1,) + (1,) * (len(extent) - 1 - dim))
    return gain


def gaussian(stream_key, dims, width, limit, split=(), kind=jnp.bfloat16):
    level = levels(stream_key, dims, split, -0.22, 0.18) if split else 1.0
    result = jax.random.normal(stream_key, dims, jnp.float32) * width * level
    return jnp.minimum(jnp.maximum(result, -limit), limit).astype(kind)


def setup_inputs(seed: int = 0) -> dict:
    splits = jax.random.split(jax.random.key(seed), 8)
    displacement = gaussian(splits[0], (3, NS, NN, ND), 1.0, 6.0, ((1, 64), (2, 8)), jnp.float32)
    velocity = gaussian(splits[1], (3, NS, NN, ND), 1.0, 6.0, ((1, 64), (2, 8)), jnp.float32)
    stiffness = jnp.clip(jnp.exp(math.log(1.3) - 1.1786549 * jax.random.uniform(splits[2], (NS, NN, ND), jnp.float32) ** levels(splits[2], (NS, NN, ND), ((0, 64), (1, 8)), -0.2, 0.2)), 0.4, 1.3)
    yield_flags = plant(jax.random.randint(splits[3], (NS // BLK, NN, ND // BLK), 0, 2), jax.random.fold_in(splits[3], 1), 0, 1).astype(jnp.int32)
    contact = plant((jax.random.randint(splits[4], (2, NS, ND), 0, 4) < 3).astype(jnp.int32), jax.random.fold_in(splits[4], 1), 0, 1)
    history = gaussian(splits[5], (2, HIST, 2, 3, ND, NS), 1.0, 6.0, ((4, 64),))
    kernel = gaussian(splits[6], (2, HIST, 3, NS), 0.3, 1.8, (), jnp.float32)
    return dict(displacement=displacement, velocity=velocity, stiffness=stiffness, yield_flags=yield_flags, contact=contact, history=history, kernel=kernel)


time_step = 0.5

def phase_tables(mode_count, first_mode, block_modes):
    node_ids = jnp.arange(mode_count, dtype=jnp.int32)[:, None]
    mode_ids = (first_mode + jnp.arange(block_modes, dtype=jnp.int32))[None, :]
    phases = (node_ids * mode_ids % mode_count).astype(jnp.float32) * (2.0 * math.pi / mode_count)
    return (jnp.cos(phases).astype(jnp.bfloat16), jnp.sin(phases).astype(jnp.bfloat16))

def blocks_expand(yield_map, block_size):
    strike_blocks, normal_layers, dip_blocks = yield_map.shape
    widened = jnp.broadcast_to(yield_map.astype(jnp.float32)[:, None, :, :, None], (strike_blocks, block_size, normal_layers, dip_blocks, block_size))
    return widened.reshape(strike_blocks * block_size, normal_layers, dip_blocks * block_size)

def laplace_single(values):
    strike_side = jnp.concatenate([values[-1:], values, values[:1]], axis=0)
    normal_side = jnp.pad(values, ((0, 0), (1, 1), (0, 0)))
    dip_padded = jnp.pad(values, ((0, 0), (0, 0), (1, 1)))
    return strike_side[2:] + strike_side[:-2] + (normal_side[:, 2:] + normal_side[:, :-2]) + (dip_padded[..., 2:] + dip_padded[..., :-2]) - 6.0 * values

def reference(displacement, velocity, stiffness, yield_flags, contact, history, kernel):
    modulus = stiffness * (1.0 - 0.5 * blocks_expand(yield_flags, BLK))
    cosines, sines = phase_tables(NS, 0, NS)
    normalizer = 1.0 / math.sqrt(NS)
    planes = jnp.stack([displacement[:, :, 0, :], displacement[:, :, NN - 1, :]]).astype(jnp.bfloat16)
    flat = jnp.swapaxes(planes, 2, 3).reshape(2 * 3 * ND, NS)
    real_part = normalizer * jnp.dot(flat, cosines, preferred_element_type=jnp.float32)
    imag_part = -(normalizer * jnp.dot(flat, sines, preferred_element_type=jnp.float32))
    current = jnp.stack([real_part.reshape(2, 3, ND, NS), imag_part.reshape(2, 3, ND, NS)], axis=1)
    lagged = jnp.concatenate([current[:, None], history[:, :-1].astype(jnp.float32)], axis=1)
    weights = kernel[:, :, None, :, None, :]
    modal_force = lax.optimization_barrier(jnp.sum(weights * lagged, axis=1)).astype(jnp.bfloat16)
    upper = modal_force[:, 0].reshape(2 * 3 * ND, NS)
    lower = modal_force[:, 1].reshape(2 * 3 * ND, NS)
    traction = normalizer * (jnp.dot(upper, cosines.T, preferred_element_type=jnp.float32) - jnp.dot(lower, sines.T, preferred_element_type=jnp.float32))
    traction = jnp.swapaxes(traction.reshape(2, 3, ND, NS), 2, 3)
    pushed = contact.astype(jnp.float32)[:, None] * traction
    force = jnp.zeros_like(displacement).at[:, :, 0, :].set(pushed[0]).at[:, :, NN - 1, :].set(pushed[1])

    def advance(items):
        moved, speed, loading = items
        for substep in range(SUB):
            acceleration = modulus * laplace_single(moved) + loading
            speed = speed + time_step * acceleration
            moved = moved + time_step * speed
        return (moved, speed)
    final_displacement, final_velocity = lax.map(advance, (displacement, velocity, force))
    return (final_displacement, final_velocity)
```

```python
import functools
import math

import jax
import jax.numpy as jnp
import numpy as np
from jax import lax
from jax.experimental import pallas as pl
from jax.experimental.pallas import tpu as pltpu
from jax.sharding import PartitionSpec as P

MESH = pl.DeviceIdType.MESH
SUB = 3
time_step = 0.5

YH, NZ, NX = 2, 8, 4
GROUP = YH * NX
SLABS = YH * NZ * NX
OWN = 32
NS = SLABS * OWN
N1, N2 = 128, 16
F32, BF16 = jnp.float32, jnp.bfloat16


def tables():
    z = np.arange(NZ)[:, None]
    b = np.arange(GROUP)[None, :]
    slab_zb = ((b // NX) * (NZ * NX) + z * NX + b % NX).reshape(-1)
    slab_bz = ((b // NX) * (NZ * NX) + z * NX + b % NX).T.reshape(-1)
    k1 = np.arange(N1)
    n2 = np.arange(N2)
    t = np.arange(N2)
    first = np.concatenate([2 * slab_bz, 2 * slab_bz + 1])
    angle = 2 * np.pi * (np.outer(first, k1) % N1) / N1
    forward = np.concatenate([np.cos(angle), -np.sin(angle)], axis=1)
    twist = 2 * np.pi * np.outer(n2, k1) / NS / 1.0
    norm = 1.0 / math.sqrt(NS)
    twiddle = norm * np.stack([np.tile(np.cos(twist), (8, 1)), np.tile(-np.sin(twist), (8, 1))])
    small = 2 * np.pi * (np.outer(t, n2) % N2) / N2
    co, si = np.cos(small), np.sin(small)
    inner = np.zeros((2, 3, 2, N2, 2, 2, 4, N2))
    outer = np.zeros((2, 2, 4, N2, 2, 3, 2, N2))
    for c in range(3):
        for dd in range(2):
            inner[0, c, dd, :, 0, dd, c, :] = co
            inner[0, c, dd, :, 1, dd, c, :] = si
            inner[1, c, dd, :, 0, dd, c, :] = -si
            inner[1, c, dd, :, 1, dd, c, :] = co
            outer[0, dd, c, :, 0, c, dd, :] = co.T
            outer[0, dd, c, :, 1, c, dd, :] = -si.T
            outer[1, dd, c, :, 0, c, dd, :] = si.T
            outer[1, dd, c, :, 1, c, dd, :] = co.T
    inner = inner.reshape(192, 256)
    outer = outer.reshape(256, 192)
    last = np.concatenate([2 * slab_zb - 1 + r for r in range(4)]) % N1
    angle = 2 * np.pi * (np.outer(last, k1) % N1) / N1
    inverse = np.concatenate([np.cos(angle), -np.sin(angle)], axis=1)
    dips = np.arange(128)[None, :]
    pack = np.stack([dips == 2 * slab_zb[:, None] + dd for dd in range(2)])
    unpack = np.stack([dips == 2 * slab_bz[:, None] + dd for dd in range(2)])
    widen = np.arange(32)[:, None] == dips // 4
    bf = [forward, inner, outer, inverse, pack, unpack, widen]
    return [jnp.asarray(a.astype(np.float32), dtype=BF16) for a in bf] + [
        jnp.asarray(twiddle.astype(np.float32))
    ]


def mm(a, b):
    return jnp.dot(a.astype(BF16), b.astype(BF16), preferred_element_type=F32)


def mm_nt(a, b):
    return lax.dot_general(
        a.astype(BF16), b.astype(BF16), (((1,), (1,)), ((), ())), preferred_element_type=F32
    )


def dip_sides(x):
    axis = x.ndim - 1
    lane = lax.broadcasted_iota(jnp.int32, x.shape, axis)
    below = jnp.where(lane == 0, 0.0, pltpu.roll(x, 1, axis))
    above = jnp.where(lane == 127, 0.0, pltpu.roll(x, 127, axis))
    return below + above


def kernel(
    u_in, v_in, stiff_in, flags_in, contact_in, past_in, newest_in,
    forward_in, inner_in, outer_in, inverse_in, pack_in, unpack_in, widen_in, twiddle_in,
    u_out, v_out,
    us0, us1, us2, uf, vs, stiff, flags, mods, contacts, past, newest,
    forward, inner, outer, inverse, pack, unpack, widen, twiddle,
    faces, sides, p1, g1, r1, p2, g2, q2, force, mod2,
    in_sem, out_sem, self_sem, halo_s, halo_r, aux_s, aux_r, a2a_s, a2a_r,
):
    s = lax.axis_index("strike")
    m = lax.axis_index("normal")
    my_z = (s // NX) % NZ
    my_b = (s // (NX * NZ)) * NX + s % NX
    low, high = m == 0, m == 7
    plane = jnp.logical_or(low, high)
    left, right = (s + SLABS - 1) % SLABS, (s + 1) % SLABS
    mine_b_base = (my_b // NX) * (NZ * NX) + my_b % NX

    def z_peer(i):
        z = (my_z + i) % NZ
        return z, mine_b_base + z * NX

    def b_peer(i):
        b = (my_b + i) % GROUP
        return b, (b // NX) * (NZ * NX) + my_z * NX + b % NX

    barrier = pltpu.get_barrier_semaphore()

    def greet(**where):
        pl.semaphore_signal(barrier, inc=1, device_id=where, device_id_type=MESH)

    greet(strike=left)
    greet(strike=right)

    @pl.when(jnp.logical_not(low))
    def _():
        greet(normal=m - 1)

    @pl.when(jnp.logical_not(high))
    def _():
        greet(normal=m + 1)

    @pl.when(plane)
    def _():
        for i in range(1, NZ):
            greet(strike=z_peer(i)[1])
        for i in range(1, GROUP):
            greet(strike=b_peer(i)[1])

    loads = [
        pltpu.make_async_copy(u_in, us0.at[:, pl.ds(1, OWN)], in_sem.at[0]),
        pltpu.make_async_copy(pack_in, pack, in_sem.at[1]),
        pltpu.make_async_copy(flags_in, flags, in_sem.at[2]),
        pltpu.make_async_copy(stiff_in, stiff, in_sem.at[3]),
        pltpu.make_async_copy(widen_in, widen, in_sem.at[4]),
        pltpu.make_async_copy(contact_in, contacts.at[pl.ds(8, OWN)], in_sem.at[5]),
        pltpu.make_async_copy(v_in, vs, in_sem.at[6]),
        pltpu.make_async_copy(forward_in, forward, in_sem.at[7]),
        pltpu.make_async_copy(inner_in, inner, in_sem.at[8]),
        pltpu.make_async_copy(outer_in, outer, in_sem.at[9]),
        pltpu.make_async_copy(inverse_in, inverse, in_sem.at[10]),
        pltpu.make_async_copy(unpack_in, unpack, in_sem.at[11]),
        pltpu.make_async_copy(twiddle_in, twiddle, in_sem.at[12]),
        pltpu.make_async_copy(past_in, past, in_sem.at[13]),
        pltpu.make_async_copy(newest_in, newest, in_sem.at[14]),
    ]
    for load in loads:
        load.start()

    def strike_copies(i, src):
        return [
            pltpu.make_async_remote_copy(
                src.at[:, OWN], src.at[:, 0], halo_s.at[i, 0], halo_r.at[i, 0],
                device_id={"strike": right}, device_id_type=MESH,
            ),
            pltpu.make_async_remote_copy(
                src.at[:, 1], src.at[:, OWN + 1], halo_s.at[i, 1], halo_r.at[i, 1],
                device_id={"strike": left}, device_id_type=MESH,
            ),
        ]

    def up_copy(i):
        return pltpu.make_async_remote_copy(
            faces.at[i, 1], sides.at[i, 0], halo_s.at[i, 2], halo_r.at[i, 2],
            device_id={"normal": m + 1}, device_id_type=MESH,
        )

    def down_copy(i):
        return pltpu.make_async_remote_copy(
            faces.at[i, 0], sides.at[i, 1], halo_s.at[i, 3], halo_r.at[i, 3],
            device_id={"normal": m - 1}, device_id_type=MESH,
        )

    def start_halo(i, src):
        for copy in strike_copies(i, src):
            copy.start()

        @pl.when(jnp.logical_not(high))
        def _():
            up_copy(i).start()

        @pl.when(jnp.logical_not(low))
        def _():
            down_copy(i).start()

    def wait_halo(i, src):
        for copy in strike_copies(i, src):
            copy.wait_recv()

        @pl.when(jnp.logical_not(low))
        def _():
            up_copy(i).wait_recv()

        @pl.when(jnp.logical_not(high))
        def _():
            down_copy(i).wait_recv()

    def finish_halo(i, src):
        for copy in strike_copies(i, src):
            copy.wait_send()

        @pl.when(jnp.logical_not(high))
        def _():
            up_copy(i).wait_send()

        @pl.when(jnp.logical_not(low))
        def _():
            down_copy(i).wait_send()

    def set_faces(i, src):
        faces[i, 0] = src[:, 1 : OWN + 1, 0, :]
        faces[i, 1] = src[:, 1 : OWN + 1, 7, :]

    aux = [
        pltpu.make_async_remote_copy(
            mods.at[OWN], mods.at[0], aux_s.at[0], aux_r.at[0],
            device_id={"strike": right}, device_id_type=MESH,
        ),
        pltpu.make_async_remote_copy(
            mods.at[1], mods.at[OWN + 1], aux_s.at[1], aux_r.at[1],
            device_id={"strike": left}, device_id_type=MESH,
        ),
        pltpu.make_async_remote_copy(
            contacts.at[pl.ds(OWN, 8)], contacts.at[pl.ds(0, 8)], aux_s.at[2], aux_r.at[2],
            device_id={"strike": right}, device_id_type=MESH,
        ),
        pltpu.make_async_remote_copy(
            contacts.at[pl.ds(8, 8)], contacts.at[pl.ds(OWN + 8, 8)], aux_s.at[3], aux_r.at[3],
            device_id={"strike": left}, device_id_type=MESH,
        ),
    ]

    def z_copies(k, src, dst):
        copies = []
        for i in range(1, NZ):
            z, who = z_peer(i)
            copies.append(
                pltpu.make_async_remote_copy(
                    src.at[z], dst.at[my_z], a2a_s.at[k, i], a2a_r.at[k, i],
                    device_id={"strike": who}, device_id_type=MESH,
                )
            )
        return copies, pltpu.make_async_copy(src.at[my_z], dst.at[my_z], self_sem.at[k])

    def b_copies(k, src, dst):
        copies = []
        for i in range(1, GROUP):
            b, who = b_peer(i)
            copies.append(
                pltpu.make_async_remote_copy(
                    src.at[:, b], dst.at[my_b], a2a_s.at[k, i], a2a_r.at[k, i],
                    device_id={"strike": who}, device_id_type=MESH,
                )
            )
        return copies, pltpu.make_async_copy(src.at[:, my_b], dst.at[my_b], self_sem.at[k])

    def launch(stage):
        for copy in stage[0]:
            copy.start()
        stage[1].start()

    def land(stage):
        for copy in stage[0]:
            copy.wait_recv()
        stage[1].wait()

    def drain(stage):
        for copy in stage[0]:
            copy.wait_send()

    stages = [z_copies(0, p1, g1), b_copies(1, g1, r1), z_copies(2, p2, g2), b_copies(3, g2, q2)]

    loads[0].wait()
    set_faces(0, us0)
    loads[1].wait()

    @pl.when(plane)
    def _():
        for jh in range(2):
            rows = []
            for c in range(3):
                part = pl.ds(16 * jh, 16)
                rows.append(jnp.where(high, faces[0, 1, c, part], faces[0, 0, c, part]))
            rows.append(jnp.zeros((16, 128), F32))
            block = jnp.concatenate(rows, axis=0)
            halves = [mm_nt(pack[dd], block) for dd in range(2)]
            p1[:, :, jh, :] = jnp.concatenate(halves, axis=1).reshape(NZ, GROUP, 128)

    @pl.when(low)
    def _():
        for i in range(SUB):
            sides[i, 0] = jnp.zeros((3, OWN, 128), F32)

    @pl.when(high)
    def _():
        for i in range(SUB):
            sides[i, 1] = jnp.zeros((3, OWN, 128), F32)

    loads[2].wait()
    loads[3].wait()
    loads[4].wait()
    marks = mm(flags[...].reshape(64, 32).astype(F32), widen[...]).reshape(8, 1, 8, 128)
    mods[1 : OWN + 1] = (stiff[...].reshape(8, 4, 8, 128) * (1.0 - 0.5 * marks)).reshape(OWN, 8, 128)
    loads[5].wait()

    @pl.when(plane)
    def _():
        pl.semaphore_wait(barrier, 3 + NZ - 1 + GROUP - 1)
        launch(stages[0])

    @pl.when(jnp.logical_not(plane))
    def _():
        pl.semaphore_wait(barrier, 4)

    start_halo(0, us0)
    for copy in aux:
        copy.start()

    def substep(i, src, dst, offset):
        for c in range(3):
            here = src[c, 1 : OWN + 1]
            layer = lax.broadcasted_iota(jnp.int32, here.shape, 1)
            below = jnp.where(layer == 0, sides[i, 0, c][:, None, :], pltpu.roll(here, 1, 1))
            above = jnp.where(layer == 7, sides[i, 1, c][:, None, :], pltpu.roll(here, 7, 1))
            lap = (
                src[c, 2 : OWN + 2] + src[c, 0:OWN] + (above + below) + dip_sides(here) - 6.0 * here
            )
            speed = vs[c] + time_step * (mods[1 : OWN + 1] * lap)
            vs[c] = speed
            dst[c, offset : offset + OWN] = here + time_step * speed

    @pl.when(plane)
    def _():
        land(stages[0])
        launch(stages[1])

    loads[6].wait()
    wait_halo(0, us0)
    substep(0, us0, us1, 1)
    set_faces(1, us1)
    start_halo(1, us1)

    for load in loads[7:]:
        load.wait()

    @pl.when(plane)
    def _():
        land(stages[1])
        got = jnp.concatenate([r1[:, :, jh, :].reshape(SLABS, 128) for jh in range(2)], axis=0)
        y = mm(got.T, forward[...])
        re, im = y[:, :128], y[:, 128:]
        tr, ti = twiddle[0], twiddle[1]
        turned = jnp.concatenate([re * tr - im * ti, re * ti + im * tr], axis=0)
        modes = mm(inner[...], turned)
        modal_force = newest[...] * modes + past[...]
        back = mm(outer[...], modal_force)
        re, im = back[:128], back[128:]
        turned = jnp.concatenate([re * tr + im * ti, im * tr - re * ti], axis=1)
        pulled = mm_nt(inverse[...], turned)
        for r in range(4):
            p2[:, :, r, :] = pulled[64 * r : 64 * r + 64].reshape(NZ, GROUP, 128)
        launch(stages[2])

    wait_halo(1, us1)
    substep(1, us1, us2, 1)
    set_faces(2, us2)
    start_halo(2, us2)

    @pl.when(plane)
    def _():
        land(stages[2])
        launch(stages[3])

    wait_halo(2, us2)
    substep(2, us2, uf, 0)
    for copy in aux:
        copy.wait_recv()

    @pl.when(plane)
    def _():
        mod2[...] = jnp.zeros_like(mod2)
        for k in range(3):
            mod2[k, 7:41] = jnp.where(high, mods[:, 7 - k, :], mods[:, k, :])
        land(stages[3])
        pieces = []
        for r in range(4):
            turned = q2[:, :, r, :].reshape(SLABS, 128).T
            pieces.append(mm(turned[:64], unpack[0]) + mm(turned[64:], unpack[1]))

        def lap2(x):
            return pltpu.roll(x, 1, 0) + pltpu.roll(x, 47, 0) + dip_sides(x) - 6.0 * x

        half = time_step
        for c in range(3):
            a = 16 * c
            load = contacts[...] * jnp.concatenate(
                [pieces[0][a + 8 : a + 16], pieces[1][a : a + 16],
                 pieces[2][a : a + 16], pieces[3][a : a + 8]],
                axis=0,
            )
            v0 = half * load
            u0 = half * v0
            v0, v1 = v0 + half * (mod2[0] * lap2(u0) + load), half * (mod2[1] * u0)
            u0, u1 = u0 + half * v0, half * v1
            v0, v1, v2 = (
                v0 + half * (mod2[0] * (lap2(u0) + u1) + load),
                v1 + half * (mod2[1] * (lap2(u1) + u0)),
                half * (mod2[2] * u1),
            )
            u0, u1, u2 = u0 + half * v0, u1 + half * v1, half * v2
            force[c, 0] = u0[8:40]
            force[c, 1] = u1[8:40]
            force[c, 2] = u2[8:40]
            force[c, 3] = v0[8:40]
            force[c, 4] = v1[8:40]
            force[c, 5] = v2[8:40]

        @pl.when(low)
        def _():
            for k in range(3):
                uf[:, :, k, :] = uf[:, :, k, :] + force[:, k]
                vs[:, :, k, :] = vs[:, :, k, :] + force[:, 3 + k]

        @pl.when(high)
        def _():
            for k in range(3):
                uf[:, :, 7 - k, :] = uf[:, :, 7 - k, :] + force[:, k]
                vs[:, :, 7 - k, :] = vs[:, :, 7 - k, :] + force[:, 3 + k]

    stores = [
        pltpu.make_async_copy(uf, u_out, out_sem.at[0]),
        pltpu.make_async_copy(vs, v_out, out_sem.at[1]),
    ]
    for store in stores:
        store.start()
    for i, src in enumerate((us0, us1, us2)):
        finish_halo(i, src)
    for copy in aux:
        copy.wait_send()

    @pl.when(plane)
    def _():
        for stage in stages:
            drain(stage)

    for store in stores:
        store.wait()


def body(displacement, velocity, stiffness, yield_flags, contact, history, kern):
    face = (lax.axis_index("normal") == lax.axis_size("normal") - 1).astype(jnp.int32)
    own_history = lax.dynamic_index_in_dim(history, face, 0, keepdims=False)
    own_kernel = lax.dynamic_index_in_dim(kern, face, 0, keepdims=False)
    touching = lax.dynamic_index_in_dim(contact, face, 0, keepdims=False).astype(F32)
    past = jnp.sum(own_kernel[1:, None, :, None, :] * own_history[:-1].astype(F32), axis=0)
    past = past.reshape(192, 128)
    newest = jnp.broadcast_to(own_kernel[0][None, :, None, :], (2, 3, 2, NS)).reshape(192, 128)
    any_space = pl.BlockSpec(memory_space=pl.ANY)
    dma, vmem = pltpu.SemaphoreType.DMA, pltpu.VMEM
    scratch = [
        vmem((3, OWN + 2, 8, 128), F32),
        vmem((3, OWN + 2, 8, 128), F32),
        vmem((3, OWN + 2, 8, 128), F32),
        vmem((3, OWN, 8, 128), F32),
        vmem((3, OWN, 8, 128), F32),
        vmem((OWN, 8, 128), F32),
        vmem((8, 8, 32), jnp.int32),
        vmem((OWN + 2, 8, 128), F32),
        vmem((OWN + 16, 128), F32),
        vmem((192, 128), F32),
        vmem((192, 128), F32),
        vmem((128, 256), BF16),
        vmem((192, 256), BF16),
        vmem((256, 192), BF16),
        vmem((256, 256), BF16),
        vmem((2, 64, 128), BF16),
        vmem((2, 64, 128), BF16),
        vmem((32, 128), BF16),
        vmem((2, 128, 128), F32),
        vmem((SUB, 2, 3, OWN, 128), F32),
        vmem((SUB, 2, 3, OWN, 128), F32),
        vmem((NZ, GROUP, 2, 128), F32),
        vmem((NZ, GROUP, 2, 128), F32),
        vmem((GROUP, NZ, 2, 128), F32),
        vmem((NZ, GROUP, 4, 128), F32),
        vmem((NZ, GROUP, 4, 128), F32),
        vmem((GROUP, NZ, 4, 128), F32),
        vmem((3, 6, OWN, 128), F32),
        vmem((3, OWN + 16, 128), F32),
        dma((15,)),
        dma((2,)),
        dma((4,)),
        dma((SUB, 4)),
        dma((SUB, 4)),
        dma((4,)),
        dma((4,)),
        dma((4, 8)),
        dma((4, 8)),
    ]
    out = jax.ShapeDtypeStruct(displacement.shape, F32)
    return pl.pallas_call(
        kernel,
        out_shape=(out, out),
        in_specs=[any_space] * 15,
        out_specs=(any_space, any_space),
        scratch_shapes=scratch,
        compiler_params=pltpu.CompilerParams(collective_id=0, has_side_effects=True),
        name="slab_step",
    )(displacement, velocity, stiffness, yield_flags, touching, past, newest, *tables())


def solution(mesh):
    return jax.shard_map(
        body,
        mesh=mesh,
        in_specs=(
            P(None, "strike", "normal", None),
            P(None, "strike", "normal", None),
            P("strike", "normal", None),
            P("strike", "normal", None),
            P(None, "strike", None),
            P(None, None, None, None, "strike", None),
            P(),
        ),
        out_specs=(P(None, "strike", "normal", None), P(None, "strike", "normal", None)),
        check_vma=False,
    )
```

```python
import functools
import math

import jax
import jax.numpy as jnp
import numpy as np
from jax import lax
from jax.experimental import pallas as pl
from jax.experimental.pallas import tpu as pltpu
from jax.sharding import PartitionSpec as P

MESH = pl.DeviceIdType.MESH
SUB = 3
time_step = 0.5

YH, NZ, NX = 2, 8, 4
GROUP = YH * NX
SLABS = YH * NZ * NX
OWN = 32
NS = SLABS * OWN
N1, N2 = 128, 16
F32, BF16 = jnp.float32, jnp.bfloat16


def tables():
    z = np.arange(NZ)[:, None]
    b = np.arange(GROUP)[None, :]
    slab_zb = ((b // NX) * (NZ * NX) + z * NX + b % NX).reshape(-1)
    slab_bz = ((b // NX) * (NZ * NX) + z * NX + b % NX).T.reshape(-1)
    k1 = np.arange(N1)
    n2 = np.arange(N2)
    t = np.arange(N2)
    first = np.concatenate([2 * slab_bz, 2 * slab_bz + 1])
    angle = 2 * np.pi * (np.outer(first, k1) % N1) / N1
    forward = np.concatenate([np.cos(angle), -np.sin(angle)], axis=1)
    twist = 2 * np.pi * np.outer(n2, k1) / NS / 1.0
    norm = 1.0 / math.sqrt(NS)
    twiddle = norm * np.stack([np.tile(np.cos(twist), (8, 1)), np.tile(-np.sin(twist), (8, 1))])
    small = 2 * np.pi * (np.outer(t, n2) % N2) / N2
    co, si = np.cos(small), np.sin(small)
    inner = np.zeros((2, 3, 2, N2, 2, 2, 4, N2))
    outer = np.zeros((2, 2, 4, N2, 2, 3, 2, N2))
    for c in range(3):
        for dd in range(2):
            inner[0, c, dd, :, 0, dd, c, :] = co
            inner[0, c, dd, :, 1, dd, c, :] = si
            inner[1, c, dd, :, 0, dd, c, :] = -si
            inner[1, c, dd, :, 1, dd, c, :] = co
            outer[0, dd, c, :, 0, c, dd, :] = co.T
            outer[0, dd, c, :, 1, c, dd, :] = -si.T
            outer[1, dd, c, :, 0, c, dd, :] = si.T
            outer[1, dd, c, :, 1, c, dd, :] = co.T
    inner = inner.reshape(192, 256)
    outer = outer.reshape(256, 192)
    last = np.concatenate([2 * slab_zb - 1 + r for r in range(4)]) % N1
    angle = 2 * np.pi * (np.outer(last, k1) % N1) / N1
    inverse = np.concatenate([np.cos(angle), -np.sin(angle)], axis=1)
    dips = np.arange(128)[None, :]
    pack = np.stack([dips == 2 * slab_zb[:, None] + dd for dd in range(2)])
    unpack = np.stack([dips == 2 * slab_bz[:, None] + dd for dd in range(2)])
    widen = np.arange(32)[:, None] == dips // 4
    bf = [forward, inner, outer, inverse, pack, unpack, widen]
    return [jnp.asarray(a.astype(np.float32), dtype=BF16) for a in bf] + [
        jnp.asarray(twiddle.astype(np.float32))
    ]


def mm(a, b):
    return jnp.dot(a.astype(BF16), b.astype(BF16), preferred_element_type=F32)


def mm_nt(a, b):
    return lax.dot_general(
        a.astype(BF16), b.astype(BF16), (((1,), (1,)), ((), ())), preferred_element_type=F32
    )


def dip_sides(x):
    axis = x.ndim - 1
    lane = lax.broadcasted_iota(jnp.int32, x.shape, axis)
    below = jnp.where(lane == 0, 0.0, pltpu.roll(x, 1, axis))
    above = jnp.where(lane == 127, 0.0, pltpu.roll(x, 127, axis))
    return below + above


def kernel(
    u_in, v_in, stiff_in, flags_in, contact_in, history_in, kern_in,
    forward_in, inner_in, outer_in, inverse_in, pack_in, unpack_in, widen_in, twiddle_in,
    uf, vs, force,
    us0, us1, us2, stiff, flags, mods, marked, contacts, history, kern, past,
    forward, inner, outer, inverse, pack, unpack, widen, twiddle,
    faces, sides, p1, g1, r1, p2, g2, q2, mod2,
    in_sem, past_sem, self_sem, halo_s, halo_r, aux_s, aux_r, a2a_s, a2a_r,
):
    s = lax.axis_index("strike")
    m = lax.axis_index("normal")
    my_z = (s // NX) % NZ
    my_b = (s // (NX * NZ)) * NX + s % NX
    low, high = m == 0, m == 7
    plane = jnp.logical_or(low, high)
    face = m // 7
    left, right = (s + SLABS - 1) % SLABS, (s + 1) % SLABS
    mine_b_base = (my_b // NX) * (NZ * NX) + my_b % NX

    def z_peer(i):
        z = (my_z + i) % NZ
        return z, mine_b_base + z * NX

    def b_peer(i):
        b = (my_b + i) % GROUP
        return b, (b // NX) * (NZ * NX) + my_z * NX + b % NX

    barrier = pltpu.get_barrier_semaphore()

    def greet(**where):
        pl.semaphore_signal(barrier, inc=1, device_id=where, device_id_type=MESH)

    greet(strike=left)
    greet(strike=right)

    @pl.when(jnp.logical_not(low))
    def _():
        greet(normal=m - 1)

    @pl.when(jnp.logical_not(high))
    def _():
        greet(normal=m + 1)

    @pl.when(plane)
    def _():
        for i in range(1, NZ):
            greet(strike=z_peer(i)[1])
        for i in range(1, GROUP):
            greet(strike=b_peer(i)[1])

    loads = [
        pltpu.make_async_copy(u_in, us0.at[:, pl.ds(1, OWN)], in_sem.at[0]),
        pltpu.make_async_copy(pack_in, pack, in_sem.at[1]),
        pltpu.make_async_copy(flags_in, flags, in_sem.at[2]),
        pltpu.make_async_copy(stiff_in, stiff, in_sem.at[3]),
        pltpu.make_async_copy(widen_in, widen, in_sem.at[4]),
        pltpu.make_async_copy(contact_in.at[face], marked, in_sem.at[5]),
        pltpu.make_async_copy(v_in, vs, in_sem.at[6]),
        pltpu.make_async_copy(forward_in, forward, in_sem.at[7]),
        pltpu.make_async_copy(inner_in, inner, in_sem.at[8]),
        pltpu.make_async_copy(outer_in, outer, in_sem.at[9]),
        pltpu.make_async_copy(inverse_in, inverse, in_sem.at[10]),
        pltpu.make_async_copy(unpack_in, unpack, in_sem.at[11]),
        pltpu.make_async_copy(twiddle_in, twiddle, in_sem.at[12]),
    ]
    for load in loads:
        load.start()
    past_loads = []
    for t in range(N2):
        lanes = pl.ds(128 * t, 128)
        past_loads += [
            pltpu.make_async_copy(
                history_in.at[face, pl.ds(0, 7), :, :, :, lanes], history.at[t], past_sem.at[0, t]
            ),
            pltpu.make_async_copy(kern_in.at[face, :, :, lanes], kern.at[t], past_sem.at[1, t]),
        ]

    @pl.when(plane)
    def _():
        for load in past_loads:
            load.start()

    def strike_copies(i, src):
        return [
            pltpu.make_async_remote_copy(
                src.at[:, OWN], src.at[:, 0], halo_s.at[i, 0], halo_r.at[i, 0],
                device_id={"strike": right}, device_id_type=MESH,
            ),
            pltpu.make_async_remote_copy(
                src.at[:, 1], src.at[:, OWN + 1], halo_s.at[i, 1], halo_r.at[i, 1],
                device_id={"strike": left}, device_id_type=MESH,
            ),
        ]

    def up_copy(i):
        return pltpu.make_async_remote_copy(
            faces.at[i, 1], sides.at[i, 0], halo_s.at[i, 2], halo_r.at[i, 2],
            device_id={"normal": m + 1}, device_id_type=MESH,
        )

    def down_copy(i):
        return pltpu.make_async_remote_copy(
            faces.at[i, 0], sides.at[i, 1], halo_s.at[i, 3], halo_r.at[i, 3],
            device_id={"normal": m - 1}, device_id_type=MESH,
        )

    def start_halo(i, src):
        for copy in strike_copies(i, src):
            copy.start()

        @pl.when(jnp.logical_not(high))
        def _():
            up_copy(i).start()

        @pl.when(jnp.logical_not(low))
        def _():
            down_copy(i).start()

    def wait_halo(i, src):
        for copy in strike_copies(i, src):
            copy.wait_recv()

        @pl.when(jnp.logical_not(low))
        def _():
            up_copy(i).wait_recv()

        @pl.when(jnp.logical_not(high))
        def _():
            down_copy(i).wait_recv()

    def finish_halo(i, src):
        for copy in strike_copies(i, src):
            copy.wait_send()

        @pl.when(jnp.logical_not(high))
        def _():
            up_copy(i).wait_send()

        @pl.when(jnp.logical_not(low))
        def _():
            down_copy(i).wait_send()

    def set_faces(i, src):
        faces[i, 0] = src[:, 1 : OWN + 1, 0, :]
        faces[i, 1] = src[:, 1 : OWN + 1, 7, :]

    aux = [
        pltpu.make_async_remote_copy(
            mods.at[OWN], mods.at[0], aux_s.at[0], aux_r.at[0],
            device_id={"strike": right}, device_id_type=MESH,
        ),
        pltpu.make_async_remote_copy(
            mods.at[1], mods.at[OWN + 1], aux_s.at[1], aux_r.at[1],
            device_id={"strike": left}, device_id_type=MESH,
        ),
        pltpu.make_async_remote_copy(
            contacts.at[pl.ds(OWN, 8)], contacts.at[pl.ds(0, 8)], aux_s.at[2], aux_r.at[2],
            device_id={"strike": right}, device_id_type=MESH,
        ),
        pltpu.make_async_remote_copy(
            contacts.at[pl.ds(8, 8)], contacts.at[pl.ds(OWN + 8, 8)], aux_s.at[3], aux_r.at[3],
            device_id={"strike": left}, device_id_type=MESH,
        ),
    ]

    def z_copies(k, src, dst):
        copies = []
        for i in range(1, NZ):
            z, who = z_peer(i)
            copies.append(
                pltpu.make_async_remote_copy(
                    src.at[z], dst.at[my_z], a2a_s.at[k, i], a2a_r.at[k, i],
                    device_id={"strike": who}, device_id_type=MESH,
                )
            )
        return copies, pltpu.make_async_copy(src.at[my_z], dst.at[my_z], self_sem.at[k])

    def b_copies(k, src, dst):
        copies = []
        for i in range(1, GROUP):
            b, who = b_peer(i)
            copies.append(
                pltpu.make_async_remote_copy(
                    src.at[:, b], dst.at[my_b], a2a_s.at[k, i], a2a_r.at[k, i],
                    device_id={"strike": who}, device_id_type=MESH,
                )
            )
        return copies, pltpu.make_async_copy(src.at[:, my_b], dst.at[my_b], self_sem.at[k])

    def launch(stage):
        for copy in stage[0]:
            copy.start()
        stage[1].start()

    def land(stage):
        for copy in stage[0]:
            copy.wait_recv()
        stage[1].wait()

    def drain(stage):
        for copy in stage[0]:
            copy.wait_send()

    stages = [z_copies(0, p1, g1), b_copies(1, g1, r1), z_copies(2, p2, g2), b_copies(3, g2, q2)]

    loads[0].wait()
    set_faces(0, us0)
    loads[1].wait()

    @pl.when(plane)
    def _():
        for jh in range(2):
            rows = []
            for c in range(3):
                part = pl.ds(16 * jh, 16)
                rows.append(jnp.where(high, faces[0, 1, c, part], faces[0, 0, c, part]))
            rows.append(jnp.zeros((16, 128), F32))
            block = jnp.concatenate(rows, axis=0)
            halves = [mm_nt(pack[dd], block) for dd in range(2)]
            p1[:, :, jh, :] = jnp.concatenate(halves, axis=1).reshape(NZ, GROUP, 128)

    @pl.when(low)
    def _():
        for i in range(SUB):
            sides[i, 0] = jnp.zeros((3, OWN, 128), F32)

    @pl.when(high)
    def _():
        for i in range(SUB):
            sides[i, 1] = jnp.zeros((3, OWN, 128), F32)

    loads[2].wait()
    loads[3].wait()
    loads[4].wait()
    marks = mm(flags[...].reshape(64, 32).astype(F32), widen[...]).reshape(8, 1, 8, 128)
    mods[1 : OWN + 1] = (stiff[...].reshape(8, 4, 8, 128) * (1.0 - 0.5 * marks)).reshape(OWN, 8, 128)
    loads[5].wait()
    contacts[8 : OWN + 8] = marked[...].astype(F32)

    @pl.when(plane)
    def _():
        pl.semaphore_wait(barrier, 3 + NZ - 1 + GROUP - 1)
        launch(stages[0])

    @pl.when(jnp.logical_not(plane))
    def _():
        pl.semaphore_wait(barrier, 4)

    start_halo(0, us0)
    for copy in aux:
        copy.start()

    @pl.when(plane)
    def _():
        for load in past_loads:
            load.wait()
        for c in range(3):
            for q in range(2):
                total = jnp.zeros((N2, 2, 128), F32)
                for lag in range(7):
                    weight = kern[:, c, lag + 1, :][:, None, :]
                    total = total + weight * history[:, lag, q, c].astype(F32)
                past[q, c] = total

    def substep(i, src, dst, offset):
        for c in range(3):
            here = src[c, 1 : OWN + 1]
            layer = lax.broadcasted_iota(jnp.int32, here.shape, 1)
            below = jnp.where(layer == 0, sides[i, 0, c][:, None, :], pltpu.roll(here, 1, 1))
            above = jnp.where(layer == 7, sides[i, 1, c][:, None, :], pltpu.roll(here, 7, 1))
            lap = (
                src[c, 2 : OWN + 2] + src[c, 0:OWN] + (above + below) + dip_sides(here) - 6.0 * here
            )
            speed = vs[c] + time_step * (mods[1 : OWN + 1] * lap)
            vs[c] = speed
            dst[c, offset : offset + OWN] = here + time_step * speed

    @pl.when(plane)
    def _():
        land(stages[0])
        launch(stages[1])

    loads[6].wait()
    wait_halo(0, us0)
    substep(0, us0, us1, 1)
    set_faces(1, us1)
    start_halo(1, us1)

    for load in loads[7:]:
        load.wait()

    @pl.when(plane)
    def _():
        land(stages[1])
        got = jnp.concatenate([r1[:, :, jh, :].reshape(SLABS, 128) for jh in range(2)], axis=0)
        y = mm(got.T, forward[...])
        re, im = y[:, :128], y[:, 128:]
        tr, ti = twiddle[0], twiddle[1]
        turned = jnp.concatenate([re * tr - im * ti, re * ti + im * tr], axis=0)
        modes = mm(inner[...], turned)
        older = jnp.concatenate(
            [past[q, c, :, dd, :] for q in range(2) for c in range(3) for dd in range(2)], axis=0
        )
        newest = jnp.concatenate([kern[:, c, 0, :] for c in range(3) for _ in range(2)], axis=0)
        newest = jnp.concatenate([newest, newest], axis=0)
        modal_force = newest * modes + older
        back = mm(outer[...], modal_force)
        re, im = back[:128], back[128:]
        turned = jnp.concatenate([re * tr + im * ti, im * tr - re * ti], axis=1)
        pulled = mm_nt(inverse[...], turned)
        for r in range(4):
            p2[:, :, r, :] = pulled[64 * r : 64 * r + 64].reshape(NZ, GROUP, 128)
        launch(stages[2])

    wait_halo(1, us1)
    substep(1, us1, us2, 1)
    set_faces(2, us2)
    start_halo(2, us2)

    @pl.when(plane)
    def _():
        land(stages[2])
        launch(stages[3])

    wait_halo(2, us2)
    substep(2, us2, uf, 0)
    for copy in aux:
        copy.wait_recv()

    @pl.when(plane)
    def _():
        mod2[...] = jnp.zeros_like(mod2)
        for k in range(3):
            mod2[k, 7:41] = jnp.where(high, mods[:, 7 - k, :], mods[:, k, :])
        land(stages[3])
        pieces = []
        for r in range(4):
            turned = q2[:, :, r, :].reshape(SLABS, 128).T
            pieces.append(mm(turned[:64], unpack[0]) + mm(turned[64:], unpack[1]))

        def lap2(x):
            return pltpu.roll(x, 1, 0) + pltpu.roll(x, 47, 0) + dip_sides(x) - 6.0 * x

        half = time_step
        for c in range(3):
            a = 16 * c
            load = contacts[...] * jnp.concatenate(
                [pieces[0][a + 8 : a + 16], pieces[1][a : a + 16],
                 pieces[2][a : a + 16], pieces[3][a : a + 8]],
                axis=0,
            )
            v0 = half * load
            u0 = half * v0
            v0, v1 = v0 + half * (mod2[0] * lap2(u0) + load), half * (mod2[1] * u0)
            u0, u1 = u0 + half * v0, half * v1
            v0, v1, v2 = (
                v0 + half * (mod2[0] * (lap2(u0) + u1) + load),
                v1 + half * (mod2[1] * (lap2(u1) + u0)),
                half * (mod2[2] * u1),
            )
            u0, u1, u2 = u0 + half * v0, u1 + half * v1, half * v2
            force[c, 0] = u0[8:40]
            force[c, 1] = u1[8:40]
            force[c, 2] = u2[8:40]
            force[c, 3] = v0[8:40]
            force[c, 4] = v1[8:40]
            force[c, 5] = v2[8:40]

    for i, src in enumerate((us0, us1, us2)):
        finish_halo(i, src)
    for copy in aux:
        copy.wait_send()

    @pl.when(plane)
    def _():
        for stage in stages:
            drain(stage)


def finish(uf, vs, force, u_out, v_out, u_new, v_new, sem):
    m = lax.axis_index("normal")
    low, high = m == 0, m == 7
    plane = jnp.logical_or(low, high)

    def store(a, b):
        copies = [
            pltpu.make_async_copy(a, u_out, sem.at[0]),
            pltpu.make_async_copy(b, v_out, sem.at[1]),
        ]
        for copy in copies:
            copy.start()
        for copy in copies:
            copy.wait()

    @pl.when(jnp.logical_not(plane))
    def _():
        store(uf, vs)

    @pl.when(plane)
    def _():
        u_new[...] = uf[...]
        v_new[...] = vs[...]

        @pl.when(low)
        def _():
            for k in range(3):
                u_new[:, :, k, :] = uf[:, :, k, :] + force[:, k]
                v_new[:, :, k, :] = vs[:, :, k, :] + force[:, 3 + k]

        @pl.when(high)
        def _():
            for k in range(3):
                u_new[:, :, 7 - k, :] = uf[:, :, 7 - k, :] + force[:, k]
                v_new[:, :, 7 - k, :] = vs[:, :, 7 - k, :] + force[:, 3 + k]

        store(u_new, v_new)


def body(displacement, velocity, stiffness, yield_flags, contact, history, kern):
    any_space = pl.BlockSpec(memory_space=pl.ANY)
    dma, vmem = pltpu.SemaphoreType.DMA, pltpu.VMEM
    scratch = [
        vmem((3, OWN + 2, 8, 128), F32),
        vmem((3, OWN + 2, 8, 128), F32),
        vmem((3, OWN + 2, 8, 128), F32),
        vmem((OWN, 8, 128), F32),
        vmem((8, 8, 32), jnp.int32),
        vmem((OWN + 2, 8, 128), F32),
        vmem((OWN, 128), jnp.int32),
        vmem((OWN + 16, 128), F32),
        vmem((N2, 7, 2, 3, 2, 128), BF16),
        vmem((N2, 3, 8, 128), F32),
        vmem((2, 3, N2, 2, 128), F32),
        vmem((128, 256), BF16),
        vmem((192, 256), BF16),
        vmem((256, 192), BF16),
        vmem((256, 256), BF16),
        vmem((2, 64, 128), BF16),
        vmem((2, 64, 128), BF16),
        vmem((32, 128), BF16),
        vmem((2, 128, 128), F32),
        vmem((SUB, 2, 3, OWN, 128), F32),
        vmem((SUB, 2, 3, OWN, 128), F32),
        vmem((NZ, GROUP, 2, 128), F32),
        vmem((NZ, GROUP, 2, 128), F32),
        vmem((GROUP, NZ, 2, 128), F32),
        vmem((NZ, GROUP, 4, 128), F32),
        vmem((NZ, GROUP, 4, 128), F32),
        vmem((GROUP, NZ, 4, 128), F32),
        vmem((3, OWN + 16, 128), F32),
        dma((13,)),
        dma((2, N2)),
        dma((4,)),
        dma((SUB, 4)),
        dma((SUB, 4)),
        dma((4,)),
        dma((4,)),
        dma((4, 8)),
        dma((4, 8)),
    ]
    out = jax.ShapeDtypeStruct(displacement.shape, F32)
    in_vmem = pl.BlockSpec(memory_space=pltpu.VMEM)
    pieces = pl.pallas_call(
        kernel,
        out_shape=(out, out, jax.ShapeDtypeStruct((3, 6, OWN, 128), F32)),
        in_specs=[any_space] * 15,
        out_specs=(in_vmem,) * 3,
        scratch_shapes=scratch,
        compiler_params=pltpu.CompilerParams(collective_id=0, has_side_effects=True),
        name="slab_step",
    )(
        displacement, velocity, stiffness, yield_flags, contact, history,
        jnp.swapaxes(kern, 1, 2), *tables(),
    )
    return pl.pallas_call(
        finish,
        out_shape=(out, out),
        in_specs=[in_vmem] * 3,
        out_specs=(any_space, any_space),
        scratch_shapes=[vmem(out.shape, F32), vmem(out.shape, F32), dma((2,))],
        name="slab_finish",
    )(*pieces)


def solution(mesh):
    return jax.shard_map(
        body,
        mesh=mesh,
        in_specs=(
            P(None, "strike", "normal", None),
            P(None, "strike", "normal", None),
            P("strike", "normal", None),
            P("strike", "normal", None),
            P(None, "strike", None),
            P(None, None, None, None, "strike", None),
            P(),
        ),
        out_specs=(P(None, "strike", "normal", None), P(None, "strike", "normal", None)),
        check_vma=False,
    )
```

```python
import functools
import math

import jax
import jax.numpy as jnp
import numpy as np
from jax import lax
from jax.experimental import pallas as pl
from jax.experimental.pallas import tpu as pltpu
from jax.sharding import PartitionSpec as P

MESH = pl.DeviceIdType.MESH
SUB = 3
time_step = 0.5

YH, NZ, NX = 2, 8, 4
GROUP = YH * NX
SLABS = YH * NZ * NX
OWN = 32
NS = SLABS * OWN
N1, N2 = 128, 16
GRANT = 16 * 2**20
F32, BF16 = jnp.float32, jnp.bfloat16


def tables():
    z = np.arange(NZ)[:, None]
    b = np.arange(GROUP)[None, :]
    slab_zb = ((b // NX) * (NZ * NX) + z * NX + b % NX).reshape(-1)
    slab_bz = ((b // NX) * (NZ * NX) + z * NX + b % NX).T.reshape(-1)
    k1 = np.arange(N1)
    n2 = np.arange(N2)
    t = np.arange(N2)
    first = np.concatenate([2 * slab_bz, 2 * slab_bz + 1])
    angle = 2 * np.pi * (np.outer(first, k1) % N1) / N1
    forward = np.concatenate([np.cos(angle), -np.sin(angle)], axis=1)
    twist = 2 * np.pi * np.outer(n2, k1) / NS
    norm = 1.0 / math.sqrt(NS)
    turn = [np.tile(np.cos(twist), (8, 1)), np.tile(-np.sin(twist), (8, 1))]
    small = 2 * np.pi * (np.outer(t, n2) % N2) / N2
    co, si = np.cos(small), np.sin(small)
    inner = np.zeros((2, 3, 2, N2, 2, 2, 4, N2))
    outer = np.zeros((2, 2, 4, N2, 2, 3, 2, N2))
    for c in range(3):
        for dd in range(2):
            inner[0, c, dd, :, 0, dd, c, :] = co
            inner[0, c, dd, :, 1, dd, c, :] = si
            inner[1, c, dd, :, 0, dd, c, :] = -si
            inner[1, c, dd, :, 1, dd, c, :] = co
            outer[0, dd, c, :, 0, c, dd, :] = co.T
            outer[0, dd, c, :, 1, c, dd, :] = -si.T
            outer[1, dd, c, :, 0, c, dd, :] = si.T
            outer[1, dd, c, :, 1, c, dd, :] = co.T
    node = np.concatenate([np.tile(n2, 3), np.zeros(N2, np.int64)])
    for i in range(12):
        c, beyond = (i % 6) // 2, (i % 2) + (16 if i >= 6 else -2)
        node[3 * N2 + i] = beyond
        edge = 2 * np.pi * ((t * beyond) % N2) / N2
        for dd in range(2):
            outer[0, dd, 3, i, 0, c, dd, :] = np.cos(edge)
            outer[0, dd, 3, i, 1, c, dd, :] = -np.sin(edge)
            outer[1, dd, 3, i, 0, c, dd, :] = np.sin(edge)
            outer[1, dd, 3, i, 1, c, dd, :] = np.cos(edge)
    untwist = 2 * np.pi * np.outer(np.tile(node, 2), k1) / NS
    twiddle = norm * np.stack(turn + [np.cos(untwist), np.sin(untwist)])
    inner = inner.reshape(192, 256)
    outer = outer.reshape(256, 192)
    last = np.concatenate([2 * slab_zb, 2 * slab_zb + 1])
    angle = 2 * np.pi * (np.outer(last, k1) % N1) / N1
    inverse = np.concatenate([np.cos(angle), -np.sin(angle)], axis=1)
    dips = np.arange(128)[None, :]
    pack = np.stack([dips == 2 * slab_zb[:, None] + dd for dd in range(2)])
    unpack = np.stack([dips == 2 * slab_bz[:, None] + dd for dd in range(2)])
    widen = np.arange(32)[:, None] == dips // 4
    bf = [forward, inner, outer, inverse, pack, unpack, widen]
    return [jnp.asarray(a.astype(np.float32), dtype=BF16) for a in bf] + [
        jnp.asarray(twiddle.astype(np.float32))
    ]


def mm(a, b):
    return jnp.dot(a.astype(BF16), b.astype(BF16), preferred_element_type=F32)


def mm_nt(a, b):
    return lax.dot_general(
        a.astype(BF16), b.astype(BF16), (((1,), (1,)), ((), ())), preferred_element_type=F32
    )


def dip_sides(x):
    axis = x.ndim - 1
    lane = lax.broadcasted_iota(jnp.int32, x.shape, axis)
    below = jnp.where(lane == 0, 0.0, pltpu.roll(x, 1, axis))
    above = jnp.where(lane == 127, 0.0, pltpu.roll(x, 127, axis))
    return below + above


def kernel(
    u_in, v_in, stiff_in, flags_in, contact_in, history_in, kern_in,
    forward_in, inner_in, outer_in, inverse_in, pack_in, unpack_in, widen_in, twiddle_in,
    uf, vs, force,
    us0, us1, us2, stiff, flags, mods, marked, contacts, history, kern, past,
    forward, inner, outer, inverse, pack, unpack, widen, twiddle,
    faces, sides, p1, g1, r1, p2, g2, q2, wide, pulls, mod2,
    in_sem, past_sem, self_sem, halo_s, halo_r, aux_s, aux_r, a2a_s, a2a_r,
):
    s = lax.axis_index("strike")
    m = lax.axis_index("normal")
    my_z = (s // NX) % NZ
    my_b = (s // (NX * NZ)) * NX + s % NX
    low, high = m == 0, m == 7
    plane = jnp.logical_or(low, high)
    face = m // 7
    left, right = (s + SLABS - 1) % SLABS, (s + 1) % SLABS
    mine_b_base = (my_b // NX) * (NZ * NX) + my_b % NX

    def z_peer(i):
        z = (my_z + i) % NZ
        return z, mine_b_base + z * NX

    def b_peer(i):
        b = (my_b + i) % GROUP
        return b, (b // NX) * (NZ * NX) + my_z * NX + b % NX

    barrier = pltpu.get_barrier_semaphore()

    def greet(**where):
        pl.semaphore_signal(barrier, inc=1, device_id=where, device_id_type=MESH)

    greet(strike=left)
    greet(strike=right)

    @pl.when(jnp.logical_not(low))
    def _():
        greet(normal=m - 1)

    @pl.when(jnp.logical_not(high))
    def _():
        greet(normal=m + 1)

    @pl.when(plane)
    def _():
        for i in range(1, NZ):
            greet(strike=z_peer(i)[1])
        for i in range(1, GROUP):
            greet(strike=b_peer(i)[1])

    loads = [
        pltpu.make_async_copy(u_in, us0.at[:, pl.ds(1, OWN)], in_sem.at[0]),
        pltpu.make_async_copy(pack_in, pack, in_sem.at[1]),
        pltpu.make_async_copy(flags_in, flags, in_sem.at[2]),
        pltpu.make_async_copy(stiff_in, stiff, in_sem.at[3]),
        pltpu.make_async_copy(widen_in, widen, in_sem.at[4]),
        pltpu.make_async_copy(contact_in.at[face], marked, in_sem.at[5]),
        pltpu.make_async_copy(v_in, vs, in_sem.at[6]),
        pltpu.make_async_copy(forward_in, forward, in_sem.at[7]),
        pltpu.make_async_copy(inner_in, inner, in_sem.at[8]),
        pltpu.make_async_copy(outer_in, outer, in_sem.at[9]),
        pltpu.make_async_copy(inverse_in, inverse, in_sem.at[10]),
        pltpu.make_async_copy(unpack_in, unpack, in_sem.at[11]),
        pltpu.make_async_copy(twiddle_in, twiddle, in_sem.at[12]),
    ]
    for load in loads:
        load.start()
    past_loads = []
    for t in range(N2):
        lanes = pl.ds(128 * t, 128)
        past_loads += [
            pltpu.make_async_copy(
                history_in.at[face, pl.ds(0, 7), :, :, :, lanes], history.at[t], past_sem.at[0, t]
            ),
            pltpu.make_async_copy(kern_in.at[face, :, :, lanes], kern.at[t], past_sem.at[1, t]),
        ]

    @pl.when(plane)
    def _():
        for load in past_loads:
            load.start()

    def strike_copies(i, src):
        return [
            pltpu.make_async_remote_copy(
                src.at[:, OWN], src.at[:, 0], halo_s.at[i, 0], halo_r.at[i, 0],
                device_id={"strike": right}, device_id_type=MESH,
            ),
            pltpu.make_async_remote_copy(
                src.at[:, 1], src.at[:, OWN + 1], halo_s.at[i, 1], halo_r.at[i, 1],
                device_id={"strike": left}, device_id_type=MESH,
            ),
        ]

    def up_copy(i):
        return pltpu.make_async_remote_copy(
            faces.at[i, 1], sides.at[i, 0], halo_s.at[i, 2], halo_r.at[i, 2],
            device_id={"normal": m + 1}, device_id_type=MESH,
        )

    def down_copy(i):
        return pltpu.make_async_remote_copy(
            faces.at[i, 0], sides.at[i, 1], halo_s.at[i, 3], halo_r.at[i, 3],
            device_id={"normal": m - 1}, device_id_type=MESH,
        )

    def start_halo(i, src):
        for copy in strike_copies(i, src):
            copy.start()

        @pl.when(jnp.logical_not(high))
        def _():
            up_copy(i).start()

        @pl.when(jnp.logical_not(low))
        def _():
            down_copy(i).start()

    def wait_halo(i, src):
        for copy in strike_copies(i, src):
            copy.wait_recv()

        @pl.when(jnp.logical_not(low))
        def _():
            up_copy(i).wait_recv()

        @pl.when(jnp.logical_not(high))
        def _():
            down_copy(i).wait_recv()

    def finish_halo(i, src):
        for copy in strike_copies(i, src):
            copy.wait_send()

        @pl.when(jnp.logical_not(high))
        def _():
            up_copy(i).wait_send()

        @pl.when(jnp.logical_not(low))
        def _():
            down_copy(i).wait_send()

    def set_faces(i, src):
        faces[i, 0] = src[:, 1 : OWN + 1, 0, :]
        faces[i, 1] = src[:, 1 : OWN + 1, 7, :]

    aux = [
        pltpu.make_async_remote_copy(
            mods.at[OWN], mods.at[0], aux_s.at[0], aux_r.at[0],
            device_id={"strike": right}, device_id_type=MESH,
        ),
        pltpu.make_async_remote_copy(
            mods.at[1], mods.at[OWN + 1], aux_s.at[1], aux_r.at[1],
            device_id={"strike": left}, device_id_type=MESH,
        ),
        pltpu.make_async_remote_copy(
            contacts.at[pl.ds(OWN, 8)], contacts.at[pl.ds(0, 8)], aux_s.at[2], aux_r.at[2],
            device_id={"strike": right}, device_id_type=MESH,
        ),
        pltpu.make_async_remote_copy(
            contacts.at[pl.ds(8, 8)], contacts.at[pl.ds(OWN + 8, 8)], aux_s.at[3], aux_r.at[3],
            device_id={"strike": left}, device_id_type=MESH,
        ),
    ]

    def z_copies(k, src, dst):
        copies = []
        for i in range(1, NZ):
            z, who = z_peer(i)
            copies.append(
                pltpu.make_async_remote_copy(
                    src.at[z], dst.at[my_z], a2a_s.at[k, i], a2a_r.at[k, i],
                    device_id={"strike": who}, device_id_type=MESH,
                )
            )
        return copies, pltpu.make_async_copy(src.at[my_z], dst.at[my_z], self_sem.at[k])

    def b_copies(k, src, dst):
        copies = []
        for i in range(1, GROUP):
            b, who = b_peer(i)
            copies.append(
                pltpu.make_async_remote_copy(
                    src.at[:, b], dst.at[my_b], a2a_s.at[k, i], a2a_r.at[k, i],
                    device_id={"strike": who}, device_id_type=MESH,
                )
            )
        return copies, pltpu.make_async_copy(src.at[:, my_b], dst.at[my_b], self_sem.at[k])

    def launch(stage):
        for copy in stage[0]:
            copy.start()
        stage[1].start()

    def land(stage):
        for copy in stage[0]:
            copy.wait_recv()
        stage[1].wait()

    def drain(stage):
        for copy in stage[0]:
            copy.wait_send()

    stages = [z_copies(0, p1, g1), b_copies(1, g1, r1), z_copies(2, p2, g2), b_copies(3, g2, q2)]

    loads[0].wait()
    set_faces(0, us0)
    loads[1].wait()

    @pl.when(plane)
    def _():
        for jh in range(2):
            rows = []
            for c in range(3):
                part = pl.ds(16 * jh, 16)
                rows.append(jnp.where(high, faces[0, 1, c, part], faces[0, 0, c, part]))
            rows.append(jnp.zeros((16, 128), F32))
            block = jnp.concatenate(rows, axis=0)
            halves = [mm_nt(pack[dd], block) for dd in range(2)]
            wide[:, :, jh, :] = jnp.concatenate(halves, axis=1).reshape(NZ, GROUP, 128)
        p1[...] = wide[...].astype(BF16)

    @pl.when(low)
    def _():
        for i in range(SUB):
            sides[i, 0] = jnp.zeros((3, OWN, 128), F32)

    @pl.when(high)
    def _():
        for i in range(SUB):
            sides[i, 1] = jnp.zeros((3, OWN, 128), F32)

    loads[2].wait()
    loads[3].wait()
    loads[4].wait()
    marks = mm(flags[...].reshape(64, 32).astype(F32), widen[...]).reshape(8, 1, 8, 128)
    mods[1 : OWN + 1] = (stiff[...].reshape(8, 4, 8, 128) * (1.0 - 0.5 * marks)).reshape(OWN, 8, 128)
    loads[5].wait()
    contacts[8 : OWN + 8] = marked[...].astype(F32)

    @pl.when(plane)
    def _():
        pl.semaphore_wait(barrier, 3 + NZ - 1 + GROUP - 1)
        launch(stages[0])

    @pl.when(jnp.logical_not(plane))
    def _():
        pl.semaphore_wait(barrier, 4)

    start_halo(0, us0)
    for copy in aux:
        copy.start()

    @pl.when(plane)
    def _():
        for load in past_loads:
            load.wait()
        for c in range(3):
            for q in range(2):
                total = jnp.zeros((N2, 2, 128), F32)
                for lag in range(7):
                    weight = kern[:, c, lag + 1, :][:, None, :]
                    total = total + weight * history[:, lag, q, c].astype(F32)
                past[q, c] = total

    def substep(i, src, dst, offset):
        for c in range(3):
            here = src[c, 1 : OWN + 1]
            layer = lax.broadcasted_iota(jnp.int32, here.shape, 1)
            below = jnp.where(layer == 0, sides[i, 0, c][:, None, :], pltpu.roll(here, 1, 1))
            above = jnp.where(layer == 7, sides[i, 1, c][:, None, :], pltpu.roll(here, 7, 1))
            lap = (
                src[c, 2 : OWN + 2] + src[c, 0:OWN] + (above + below) + dip_sides(here) - 6.0 * here
            )
            speed = vs[c] + time_step * (mods[1 : OWN + 1] * lap)
            vs[c] = speed
            dst[c, offset : offset + OWN] = here + time_step * speed

    @pl.when(plane)
    def _():
        land(stages[0])
        launch(stages[1])

    loads[6].wait()
    wait_halo(0, us0)
    substep(0, us0, us1, 1)
    set_faces(1, us1)
    start_halo(1, us1)

    for load in loads[7:]:
        load.wait()

    @pl.when(plane)
    def _():
        land(stages[1])
        wide[...] = r1[...].astype(F32)
        got = jnp.concatenate([wide[:, :, jh, :].reshape(SLABS, 128) for jh in range(2)], axis=0)
        y = mm(got.T, forward[...])
        re, im = y[:, :128], y[:, 128:]
        tr, ti = twiddle[0], twiddle[1]
        turned = jnp.concatenate([re * tr - im * ti, re * ti + im * tr], axis=0)
        modes = mm(inner[...], turned)
        older = jnp.concatenate(
            [past[q, c, :, dd, :] for q in range(2) for c in range(3) for dd in range(2)], axis=0
        )
        newest = jnp.concatenate([kern[:, c, 0, :] for c in range(3) for _ in range(2)], axis=0)
        newest = jnp.concatenate([newest, newest], axis=0)
        modal_force = newest * modes + older
        back = mm(outer[...], modal_force)
        re, im = back[:128], back[128:]
        tr, ti = twiddle[2], twiddle[3]
        turned = jnp.concatenate([re * tr - im * ti, re * ti + im * tr], axis=1)
        pulled = mm_nt(inverse[...], turned)
        for jh in range(2):
            wide[:, :, jh, :] = pulled[64 * jh : 64 * jh + 64].reshape(NZ, GROUP, 128)
        p2[...] = wide[...].astype(BF16)
        launch(stages[2])

    wait_halo(1, us1)
    substep(1, us1, us2, 1)
    set_faces(2, us2)
    start_halo(2, us2)

    @pl.when(plane)
    def _():
        land(stages[2])
        launch(stages[3])

    wait_halo(2, us2)
    substep(2, us2, uf, 0)
    for copy in aux:
        copy.wait_recv()

    @pl.when(plane)
    def _():
        mod2[...] = jnp.zeros_like(mod2)
        pulls[...] = jnp.zeros_like(pulls)
        for k in range(3):
            mod2[k, 7:41] = jnp.where(high, mods[:, 7 - k, :], mods[:, k, :])
        land(stages[3])
        wide[...] = q2[...].astype(F32)
        pieces = []
        for jh in range(2):
            turned = wide[:, :, jh, :].reshape(SLABS, 128).T
            pieces.append(mm(turned[:64], unpack[0]) + mm(turned[64:], unpack[1]))

        def lap2(x):
            return pltpu.roll(x, 1, 0) + pltpu.roll(x, 47, 0) + dip_sides(x) - 6.0 * x

        half = time_step
        for c in range(3):
            a = 16 * c
            pulls[c, 6:8] = pieces[0][48 + 2 * c : 50 + 2 * c]
            pulls[c, 8:24] = pieces[0][a : a + 16]
            pulls[c, 24:40] = pieces[1][a : a + 16]
            pulls[c, 40:42] = pieces[1][54 + 2 * c : 56 + 2 * c]
            load = contacts[...] * pulls[c]
            v0 = half * load
            u0 = half * v0
            v0, v1 = v0 + half * (mod2[0] * lap2(u0) + load), half * (mod2[1] * u0)
            u0, u1 = u0 + half * v0, half * v1
            v0, v1, v2 = (
                v0 + half * (mod2[0] * (lap2(u0) + u1) + load),
                v1 + half * (mod2[1] * (lap2(u1) + u0)),
                half * (mod2[2] * u1),
            )
            u0, u1, u2 = u0 + half * v0, u1 + half * v1, half * v2
            force[c, 0] = u0[8:40]
            force[c, 1] = u1[8:40]
            force[c, 2] = u2[8:40]
            force[c, 3] = v0[8:40]
            force[c, 4] = v1[8:40]
            force[c, 5] = v2[8:40]

    for i, src in enumerate((us0, us1, us2)):
        finish_halo(i, src)
    for copy in aux:
        copy.wait_send()

    @pl.when(plane)
    def _():
        for stage in stages:
            drain(stage)


def finish(uf, vs, force, u_out, v_out, u_new, v_new, sem):
    m = lax.axis_index("normal")
    low, high = m == 0, m == 7
    plane = jnp.logical_or(low, high)

    def store(a, b):
        copies = [
            pltpu.make_async_copy(a, u_out, sem.at[0]),
            pltpu.make_async_copy(b, v_out, sem.at[1]),
        ]
        for copy in copies:
            copy.start()
        for copy in copies:
            copy.wait()

    @pl.when(jnp.logical_not(plane))
    def _():
        store(uf, vs)

    @pl.when(plane)
    def _():
        u_new[...] = uf[...]
        v_new[...] = vs[...]

        @pl.when(low)
        def _():
            for k in range(3):
                u_new[:, :, k, :] = uf[:, :, k, :] + force[:, k]
                v_new[:, :, k, :] = vs[:, :, k, :] + force[:, 3 + k]

        @pl.when(high)
        def _():
            for k in range(3):
                u_new[:, :, 7 - k, :] = uf[:, :, 7 - k, :] + force[:, k]
                v_new[:, :, 7 - k, :] = vs[:, :, 7 - k, :] + force[:, 3 + k]

        store(u_new, v_new)


def body(displacement, velocity, stiffness, yield_flags, contact, history, kern):
    any_space = pl.BlockSpec(memory_space=pl.ANY)
    dma, vmem = pltpu.SemaphoreType.DMA, pltpu.VMEM
    scratch = [
        vmem((3, OWN + 2, 8, 128), F32),
        vmem((3, OWN + 2, 8, 128), F32),
        vmem((3, OWN + 2, 8, 128), F32),
        vmem((OWN, 8, 128), F32),
        vmem((8, 8, 32), jnp.int32),
        vmem((OWN + 2, 8, 128), F32),
        vmem((OWN, 128), jnp.int32),
        vmem((OWN + 16, 128), F32),
        vmem((N2, 7, 2, 3, 2, 128), BF16),
        vmem((N2, 3, 8, 128), F32),
        vmem((2, 3, N2, 2, 128), F32),
        vmem((128, 256), BF16),
        vmem((192, 256), BF16),
        vmem((256, 192), BF16),
        vmem((128, 256), BF16),
        vmem((2, 64, 128), BF16),
        vmem((2, 64, 128), BF16),
        vmem((32, 128), BF16),
        vmem((4, 128, 128), F32),
        vmem((SUB, 2, 3, OWN, 128), F32),
        vmem((SUB, 2, 3, OWN, 128), F32),
        vmem((NZ, GROUP, 2, 128), BF16),
        vmem((NZ, GROUP, 2, 128), BF16),
        vmem((GROUP, NZ, 2, 128), BF16),
        vmem((NZ, GROUP, 2, 128), BF16),
        vmem((NZ, GROUP, 2, 128), BF16),
        vmem((GROUP, NZ, 2, 128), BF16),
        vmem((NZ, GROUP, 2, 128), F32),
        vmem((3, OWN + 16, 128), F32),
        vmem((3, OWN + 16, 128), F32),
        dma((13,)),
        dma((2, N2)),
        dma((4,)),
        dma((SUB, 4)),
        dma((SUB, 4)),
        dma((4,)),
        dma((4,)),
        dma((4, 8)),
        dma((4, 8)),
    ]
    out = jax.ShapeDtypeStruct(displacement.shape, F32)
    in_vmem = pl.BlockSpec(memory_space=pltpu.VMEM)
    fix = lambda x: pltpu.with_memory_space_constraint(x, pltpu.HBM)
    pieces = pl.pallas_call(
        kernel,
        out_shape=(out, out, jax.ShapeDtypeStruct((3, 6, OWN, 128), F32)),
        in_specs=[any_space] * 15,
        out_specs=(in_vmem,) * 3,
        scratch_shapes=scratch,
        compiler_params=pltpu.CompilerParams(
            collective_id=0, has_side_effects=True, vmem_limit_bytes=GRANT
        ),
        name="slab_step",
    )(
        *map(fix, (displacement, velocity, stiffness, yield_flags, contact, history)),
        fix(jnp.swapaxes(kern, 1, 2)), *map(fix, tables()),
    )
    return pl.pallas_call(
        finish,
        out_shape=(out, out),
        in_specs=[in_vmem] * 3,
        out_specs=(any_space, any_space),
        scratch_shapes=[vmem(out.shape, F32), vmem(out.shape, F32), dma((2,))],
        compiler_params=pltpu.CompilerParams(vmem_limit_bytes=GRANT),
        name="slab_finish",
    )(*pieces)


def solution(mesh):
    return jax.shard_map(
        body,
        mesh=mesh,
        in_specs=(
            P(None, "strike", "normal", None),
            P(None, "strike", "normal", None),
            P("strike", "normal", None),
            P("strike", "normal", None),
            P(None, "strike", None),
            P(None, None, None, None, "strike", None),
            P(),
        ),
        out_specs=(P(None, "strike", "normal", None), P(None, "strike", "normal", None)),
        check_vma=False,
    )
```

```python
import functools
import math

import jax
import jax.numpy as jnp
import numpy as np
from jax import lax
from jax.experimental import pallas as pl
from jax.experimental.pallas import tpu as pltpu
from jax.sharding import PartitionSpec as P

MESH = pl.DeviceIdType.MESH
SUB = 3
time_step = 0.5

YH, NZ, NX = 2, 8, 4
GROUP = YH * NX
SLABS = YH * NZ * NX
OWN = 32
NS = SLABS * OWN
N1, N2 = 128, 16
GRANT = 16 * 2**20
F32, BF16 = jnp.float32, jnp.bfloat16


def tables():
    z = np.arange(NZ)[:, None]
    b = np.arange(GROUP)[None, :]
    slab_zb = ((b // NX) * (NZ * NX) + z * NX + b % NX).reshape(-1)
    x4, h2, z8 = np.arange(NX), np.arange(YH), np.arange(NZ)
    slab_xhz = (h2[None, :, None] * (NZ * NX) + z8 * NX + x4[:, None, None]).reshape(-1)
    slab_xzh = (h2 * (NZ * NX) + z8[None, :, None] * NX + x4[:, None, None]).reshape(-1)
    k1 = np.arange(N1)
    n2 = np.arange(N2)
    t = np.arange(N2)
    first = np.concatenate([2 * slab_zb, 2 * slab_zb + 1])
    angle = 2 * np.pi * (np.outer(first, k1) % N1) / N1
    forward = np.concatenate([np.cos(angle), -np.sin(angle)], axis=1)
    twist = 2 * np.pi * np.outer(n2, k1) / NS
    norm = 1.0 / math.sqrt(NS)
    turn = [np.tile(np.cos(twist), (8, 1)), np.tile(-np.sin(twist), (8, 1))]
    small = 2 * np.pi * (np.outer(t, n2) % N2) / N2
    co, si = np.cos(small), np.sin(small)
    inner = np.zeros((2, 3, 2, N2, 2, 2, 4, N2))
    outer = np.zeros((2, 2, 4, N2, 2, 3, 2, N2))
    for c in range(3):
        for dd in range(2):
            inner[0, c, dd, :, 0, dd, c, :] = co
            inner[0, c, dd, :, 1, dd, c, :] = si
            inner[1, c, dd, :, 0, dd, c, :] = -si
            inner[1, c, dd, :, 1, dd, c, :] = co
            outer[0, dd, c, :, 0, c, dd, :] = co.T
            outer[0, dd, c, :, 1, c, dd, :] = -si.T
            outer[1, dd, c, :, 0, c, dd, :] = si.T
            outer[1, dd, c, :, 1, c, dd, :] = co.T
    node = np.concatenate([np.tile(n2, 3), np.zeros(N2, np.int64)])
    for i in range(12):
        c, beyond = (i % 6) // 2, (i % 2) + (16 if i >= 6 else -2)
        node[3 * N2 + i] = beyond
        edge = 2 * np.pi * ((t * beyond) % N2) / N2
        for dd in range(2):
            outer[0, dd, 3, i, 0, c, dd, :] = np.cos(edge)
            outer[0, dd, 3, i, 1, c, dd, :] = -np.sin(edge)
            outer[1, dd, 3, i, 0, c, dd, :] = np.sin(edge)
            outer[1, dd, 3, i, 1, c, dd, :] = np.cos(edge)
    untwist = 2 * np.pi * np.outer(np.tile(node, 2), k1) / NS
    twiddle = norm * np.stack(turn + [np.cos(untwist), np.sin(untwist)])
    inner = inner.reshape(192, 256)
    outer = outer.reshape(256, 192)
    last = np.concatenate([2 * slab_zb, 2 * slab_zb + 1])
    angle = 2 * np.pi * (np.outer(last, k1) % N1) / N1
    inverse = np.concatenate([np.cos(angle), -np.sin(angle)], axis=1)
    dips = np.arange(128)[None, :]
    pack = np.stack([dips == 2 * slab_xhz[:, None] + dd for dd in range(2)])
    unpack = np.stack([dips == 2 * slab_xzh[:, None] + dd for dd in range(2)])
    widen = np.arange(32)[:, None] == dips // 4
    bf = [forward, inner, outer, inverse, pack, unpack, widen]
    return [jnp.asarray(a.astype(np.float32), dtype=BF16) for a in bf] + [
        jnp.asarray(twiddle.astype(np.float32))
    ]


def mm(a, b):
    return jnp.dot(a.astype(BF16), b.astype(BF16), preferred_element_type=F32)


def mm_nt(a, b):
    return lax.dot_general(
        a.astype(BF16), b.astype(BF16), (((1,), (1,)), ((), ())), preferred_element_type=F32
    )


def dip_sides(x):
    axis = x.ndim - 1
    lane = lax.broadcasted_iota(jnp.int32, x.shape, axis)
    below = jnp.where(lane == 0, 0.0, pltpu.roll(x, 1, axis))
    above = jnp.where(lane == 127, 0.0, pltpu.roll(x, 127, axis))
    return below + above


def kernel(
    u_in, v_in, stiff_in, flags_in, contact_in, history_in, kern_in,
    forward_in, inner_in, outer_in, inverse_in, pack_in, unpack_in, widen_in, twiddle_in,
    uf, vs, force,
    us0, us1, us2, stiff, flags, mods, marked, contacts, history, kern, past,
    forward, inner, outer, inverse, pack, unpack, widen, twiddle,
    faces, sides, p1, g1, r1, p2, g2, q2, wide, pulls, mod2,
    in_sem, past_sem, self_sem, halo_s, halo_r, aux_s, aux_r, a2a_s, a2a_r,
):
    s = lax.axis_index("strike")
    m = lax.axis_index("normal")
    my_z = (s // NX) % NZ
    my_b = (s // (NX * NZ)) * NX + s % NX
    low, high = m == 0, m == 7
    plane = jnp.logical_or(low, high)
    face = m // 7
    left, right = (s + SLABS - 1) % SLABS, (s + 1) % SLABS
    mine_b_base = (my_b // NX) * (NZ * NX) + my_b % NX
    my_x = s % NX
    early = my_b < NX
    owner = jnp.logical_and(plane, early)
    feeder = jnp.logical_and(plane, jnp.logical_not(early))

    def x_peer(i):
        x = (my_x + i) % NX
        return x, my_z * NX + x

    def z_peer(i):
        z = (my_z + i) % NZ
        return z, mine_b_base + z * NX

    def b_peer(i):
        b = (my_b + i) % GROUP
        return b, (b // NX) * (NZ * NX) + my_z * NX + b % NX

    barrier = pltpu.get_barrier_semaphore()

    def greet(**where):
        pl.semaphore_signal(barrier, inc=1, device_id=where, device_id_type=MESH)

    greet(strike=left)
    greet(strike=right)

    @pl.when(jnp.logical_not(low))
    def _():
        greet(normal=m - 1)

    @pl.when(jnp.logical_not(high))
    def _():
        greet(normal=m + 1)

    @pl.when(owner)
    def _():
        for i in range(1, NZ):
            greet(strike=z_peer(i)[1])
        for i in range(1, GROUP):
            greet(strike=b_peer(i)[1])

    @pl.when(feeder)
    def _():
        for i in range(NX):
            greet(strike=x_peer(i)[1])

    loads = [
        pltpu.make_async_copy(u_in, us0.at[:, pl.ds(1, OWN)], in_sem.at[0]),
        pltpu.make_async_copy(pack_in, pack, in_sem.at[1]),
        pltpu.make_async_copy(flags_in, flags, in_sem.at[2]),
        pltpu.make_async_copy(stiff_in, stiff, in_sem.at[3]),
        pltpu.make_async_copy(widen_in, widen, in_sem.at[4]),
        pltpu.make_async_copy(contact_in.at[face], marked, in_sem.at[5]),
        pltpu.make_async_copy(v_in, vs, in_sem.at[6]),
        pltpu.make_async_copy(forward_in, forward, in_sem.at[7]),
        pltpu.make_async_copy(inner_in, inner, in_sem.at[8]),
        pltpu.make_async_copy(outer_in, outer, in_sem.at[9]),
        pltpu.make_async_copy(inverse_in, inverse, in_sem.at[10]),
        pltpu.make_async_copy(unpack_in, unpack, in_sem.at[11]),
        pltpu.make_async_copy(twiddle_in, twiddle, in_sem.at[12]),
    ]
    for load in loads:
        load.start()
    past_loads = []
    for t in range(N2):
        lanes = pl.ds(128 * t, 128)
        past_loads += [
            pltpu.make_async_copy(
                history_in.at[face, pl.ds(0, 7), :, :, :, lanes], history.at[t], past_sem.at[0, t]
            ),
            pltpu.make_async_copy(kern_in.at[face, :, :, lanes], kern.at[t], past_sem.at[1, t]),
        ]

    @pl.when(plane)
    def _():
        for load in past_loads:
            load.start()

    def strike_copies(i, src):
        return [
            pltpu.make_async_remote_copy(
                src.at[:, OWN], src.at[:, 0], halo_s.at[i, 0], halo_r.at[i, 0],
                device_id={"strike": right}, device_id_type=MESH,
            ),
            pltpu.make_async_remote_copy(
                src.at[:, 1], src.at[:, OWN + 1], halo_s.at[i, 1], halo_r.at[i, 1],
                device_id={"strike": left}, device_id_type=MESH,
            ),
        ]

    def up_copy(i):
        return pltpu.make_async_remote_copy(
            faces.at[i, 1], sides.at[i, 0], halo_s.at[i, 2], halo_r.at[i, 2],
            device_id={"normal": m + 1}, device_id_type=MESH,
        )

    def down_copy(i):
        return pltpu.make_async_remote_copy(
            faces.at[i, 0], sides.at[i, 1], halo_s.at[i, 3], halo_r.at[i, 3],
            device_id={"normal": m - 1}, device_id_type=MESH,
        )

    def start_halo(i, src):
        for copy in strike_copies(i, src):
            copy.start()

        @pl.when(jnp.logical_not(high))
        def _():
            up_copy(i).start()

        @pl.when(jnp.logical_not(low))
        def _():
            down_copy(i).start()

    def wait_halo(i, src):
        for copy in strike_copies(i, src):
            copy.wait_recv()

        @pl.when(jnp.logical_not(low))
        def _():
            up_copy(i).wait_recv()

        @pl.when(jnp.logical_not(high))
        def _():
            down_copy(i).wait_recv()

    def finish_halo(i, src):
        for copy in strike_copies(i, src):
            copy.wait_send()

        @pl.when(jnp.logical_not(high))
        def _():
            up_copy(i).wait_send()

        @pl.when(jnp.logical_not(low))
        def _():
            down_copy(i).wait_send()

    def set_faces(i, src):
        faces[i, 0] = src[:, 1 : OWN + 1, 0, :]
        faces[i, 1] = src[:, 1 : OWN + 1, 7, :]

    aux = [
        pltpu.make_async_remote_copy(
            mods.at[OWN], mods.at[0], aux_s.at[0], aux_r.at[0],
            device_id={"strike": right}, device_id_type=MESH,
        ),
        pltpu.make_async_remote_copy(
            mods.at[1], mods.at[OWN + 1], aux_s.at[1], aux_r.at[1],
            device_id={"strike": left}, device_id_type=MESH,
        ),
        pltpu.make_async_remote_copy(
            contacts.at[pl.ds(OWN, 8)], contacts.at[pl.ds(0, 8)], aux_s.at[2], aux_r.at[2],
            device_id={"strike": right}, device_id_type=MESH,
        ),
        pltpu.make_async_remote_copy(
            contacts.at[pl.ds(8, 8)], contacts.at[pl.ds(OWN + 8, 8)], aux_s.at[3], aux_r.at[3],
            device_id={"strike": left}, device_id_type=MESH,
        ),
    ]

    def send(k, i, j, src, dst, who):
        return pltpu.make_async_remote_copy(
            src, dst, a2a_s.at[k, i], a2a_r.at[k, j],
            device_id={"strike": who}, device_id_type=MESH,
        )

    def gather_sends(first):
        return [
            send(0, i, my_b, p1.at[x_peer(i)[0]], g1.at[my_b], x_peer(i)[1])
            for i in range(first, NX)
        ]

    def gather_self():
        return pltpu.make_async_copy(p1.at[my_x], g1.at[my_b], self_sem.at[0])

    def gather_lands():
        return [
            send(0, 0, b_peer(i)[0], p1.at[0], g1.at[b_peer(i)[0]], s ^ 1)
            for i in range(1, GROUP)
        ]

    def turn_sends():
        return [
            send(1, i, i, g1.at[:, :, z_peer(i)[0]], r1.at[my_z], z_peer(i)[1])
            for i in range(1, NZ)
        ]

    def turn_self():
        return pltpu.make_async_copy(g1.at[:, :, my_z], r1.at[my_z], self_sem.at[1])

    def return_sends():
        return [
            send(2, i, i, p2.at[z_peer(i)[0]], g2.at[my_z], z_peer(i)[1]) for i in range(1, NZ)
        ]

    def return_self():
        return pltpu.make_async_copy(p2.at[my_z], g2.at[my_z], self_sem.at[2])

    def scatter_sends():
        return [
            send(3, i, my_x, g2.at[:, b_peer(i)[0]], q2.at[my_x], b_peer(i)[1])
            for i in range(1, GROUP)
        ]

    def scatter_self():
        return pltpu.make_async_copy(g2.at[:, my_b], q2.at[my_x], self_sem.at[3])

    def scatter_lands(first):
        return [
            send(3, 0, x_peer(i)[0], g2.at[:, 0], q2.at[x_peer(i)[0]], s ^ 1)
            for i in range(first, NX)
        ]

    def past_copy(who):
        return pltpu.make_async_remote_copy(
            past.at[0], past.at[1], aux_s.at[4], aux_r.at[4],
            device_id={"strike": who}, device_id_type=MESH,
        )

    def start_all(copies):
        for copy in copies:
            copy.start()

    def recv_all(copies):
        for copy in copies:
            copy.wait_recv()

    def sent_all(copies):
        for copy in copies:
            copy.wait_send()

    loads[0].wait()
    set_faces(0, us0)
    loads[1].wait()

    @pl.when(plane)
    def _():
        for jh in range(2):
            rows = []
            for c in range(3):
                part = pl.ds(16 * jh, 16)
                rows.append(jnp.where(high, faces[0, 1, c, part], faces[0, 0, c, part]))
            rows.append(jnp.zeros((16, 128), F32))
            block = jnp.concatenate(rows, axis=0)
            halves = [mm_nt(pack[dd], block) for dd in range(2)]
            wide[:, :, jh, :] = jnp.concatenate(halves, axis=1).reshape(NZ, GROUP, 128)
        p1[...] = wide[...].reshape(NX, YH, NZ, 2, 128).astype(BF16)

    @pl.when(low)
    def _():
        for i in range(SUB):
            sides[i, 0] = jnp.zeros((3, OWN, 128), F32)

    @pl.when(high)
    def _():
        for i in range(SUB):
            sides[i, 1] = jnp.zeros((3, OWN, 128), F32)

    loads[2].wait()
    loads[3].wait()
    loads[4].wait()
    marks = mm(flags[...].reshape(64, 32).astype(F32), widen[...]).reshape(8, 1, 8, 128)
    mods[1 : OWN + 1] = (stiff[...].reshape(8, 4, 8, 128) * (1.0 - 0.5 * marks)).reshape(OWN, 8, 128)
    loads[5].wait()
    contacts[8 : OWN + 8] = marked[...].astype(F32)

    @pl.when(owner)
    def _():
        pl.semaphore_wait(barrier, 3 + NZ - 1 + GROUP - 1)
        start_all(gather_sends(1))
        gather_self().start()

    @pl.when(feeder)
    def _():
        pl.semaphore_wait(barrier, 3 + NX)
        start_all(gather_sends(0))

    @pl.when(jnp.logical_not(plane))
    def _():
        pl.semaphore_wait(barrier, 4)

    start_halo(0, us0)
    for copy in aux:
        copy.start()

    @pl.when(plane)
    def _():
        for load in past_loads:
            load.wait()
        for c in range(3):
            for q in range(2):
                total = jnp.zeros((N2, 2, 128), F32)
                for lag in range(7):
                    weight = kern[:, c, lag + 1, :][:, None, :]
                    total = total + weight * history[:, lag, q, c].astype(F32)
                past[0, q, c] = total

    @pl.when(feeder)
    def _():
        past_copy(s - NZ * NX).start()

    def substep(i, src, dst, offset):
        for c in range(3):
            here = src[c, 1 : OWN + 1]
            layer = lax.broadcasted_iota(jnp.int32, here.shape, 1)
            below = jnp.where(layer == 0, sides[i, 0, c][:, None, :], pltpu.roll(here, 1, 1))
            above = jnp.where(layer == 7, sides[i, 1, c][:, None, :], pltpu.roll(here, 7, 1))
            lap = (
                src[c, 2 : OWN + 2] + src[c, 0:OWN] + (above + below) + dip_sides(here) - 6.0 * here
            )
            speed = vs[c] + time_step * (mods[1 : OWN + 1] * lap)
            vs[c] = speed
            dst[c, offset : offset + OWN] = here + time_step * speed

    @pl.when(owner)
    def _():
        recv_all(gather_lands())
        gather_self().wait()
        start_all(turn_sends())
        turn_self().start()

    loads[6].wait()
    wait_halo(0, us0)
    substep(0, us0, us1, 1)
    set_faces(1, us1)
    start_halo(1, us1)

    for load in loads[7:]:
        load.wait()

    @pl.when(owner)
    def _():
        newest = jnp.concatenate([kern[:, c, 0, :] for c in range(3) for _ in range(2)], axis=0)
        newest = jnp.concatenate([newest, newest], axis=0)
        recv_all(turn_sends())
        turn_self().wait()
        past_copy(s ^ 1).wait_recv()
        for h in range(YH):
            wide[...] = r1[:, :, h].astype(F32)
            got = jnp.concatenate(
                [wide[:, :, jh, :].reshape(SLABS, 128) for jh in range(2)], axis=0
            )
            y = mm(got.T, forward[...])
            re, im = y[:, :128], y[:, 128:]
            tr, ti = twiddle[0], twiddle[1]
            turned = jnp.concatenate([re * tr - im * ti, re * ti + im * tr], axis=0)
            modes = mm(inner[...], turned)
            older = jnp.concatenate(
                [past[h, q, c, :, dd, :] for q in range(2) for c in range(3) for dd in range(2)],
                axis=0,
            )
            back = mm(outer[...], newest * modes + older)
            re, im = back[:128], back[128:]
            tr, ti = twiddle[2], twiddle[3]
            turned = jnp.concatenate([re * tr - im * ti, re * ti + im * tr], axis=1)
            pulled = mm_nt(inverse[...], turned)
            for jh in range(2):
                wide[:, :, jh, :] = pulled[64 * jh : 64 * jh + 64].reshape(NZ, GROUP, 128)
            p2[:, :, h] = wide[...].astype(BF16)
        start_all(return_sends())
        return_self().start()
        recv_all(return_sends())
        return_self().wait()
        start_all(scatter_sends())
        scatter_self().start()

    wait_halo(1, us1)
    substep(1, us1, us2, 1)
    set_faces(2, us2)
    start_halo(2, us2)

    wait_halo(2, us2)
    substep(2, us2, uf, 0)
    for copy in aux:
        copy.wait_recv()

    @pl.when(plane)
    def _():
        mod2[...] = jnp.zeros_like(mod2)
        pulls[...] = jnp.zeros_like(pulls)
        for k in range(3):
            mod2[k, 7:41] = jnp.where(high, mods[:, 7 - k, :], mods[:, k, :])

    @pl.when(owner)
    def _():
        recv_all(scatter_lands(1))
        scatter_self().wait()

    @pl.when(feeder)
    def _():
        recv_all(scatter_lands(0))

    @pl.when(plane)
    def _():
        wide[...] = q2[...].astype(F32).reshape(NZ, GROUP, 2, 128)
        pieces = []
        for jh in range(2):
            turned = wide[:, :, jh, :].reshape(SLABS, 128).T
            pieces.append(mm(turned[:64], unpack[0]) + mm(turned[64:], unpack[1]))

        def lap2(x):
            return pltpu.roll(x, 1, 0) + pltpu.roll(x, 47, 0) + dip_sides(x) - 6.0 * x

        half = time_step
        for c in range(3):
            a = 16 * c
            pulls[c, 6:8] = pieces[0][48 + 2 * c : 50 + 2 * c]
            pulls[c, 8:24] = pieces[0][a : a + 16]
            pulls[c, 24:40] = pieces[1][a : a + 16]
            pulls[c, 40:42] = pieces[1][54 + 2 * c : 56 + 2 * c]
            load = contacts[...] * pulls[c]
            v0 = half * load
            u0 = half * v0
            v0, v1 = v0 + half * (mod2[0] * lap2(u0) + load), half * (mod2[1] * u0)
            u0, u1 = u0 + half * v0, half * v1
            v0, v1, v2 = (
                v0 + half * (mod2[0] * (lap2(u0) + u1) + load),
                v1 + half * (mod2[1] * (lap2(u1) + u0)),
                half * (mod2[2] * u1),
            )
            u0, u1, u2 = u0 + half * v0, u1 + half * v1, half * v2
            force[c, 0] = u0[8:40]
            force[c, 1] = u1[8:40]
            force[c, 2] = u2[8:40]
            force[c, 3] = v0[8:40]
            force[c, 4] = v1[8:40]
            force[c, 5] = v2[8:40]

    for i, src in enumerate((us0, us1, us2)):
        finish_halo(i, src)
    for copy in aux:
        copy.wait_send()

    @pl.when(owner)
    def _():
        sent_all(gather_sends(1) + turn_sends() + return_sends() + scatter_sends())

    @pl.when(feeder)
    def _():
        sent_all(gather_sends(0))
        past_copy(s - NZ * NX).wait_send()


def finish(uf, vs, force, u_out, v_out, u_new, v_new, sem):
    m = lax.axis_index("normal")
    low, high = m == 0, m == 7
    plane = jnp.logical_or(low, high)

    def store(a, b):
        copies = [
            pltpu.make_async_copy(a, u_out, sem.at[0]),
            pltpu.make_async_copy(b, v_out, sem.at[1]),
        ]
        for copy in copies:
            copy.start()
        for copy in copies:
            copy.wait()

    @pl.when(jnp.logical_not(plane))
    def _():
        store(uf, vs)

    @pl.when(plane)
    def _():
        u_new[...] = uf[...]
        v_new[...] = vs[...]

        @pl.when(low)
        def _():
            for k in range(3):
                u_new[:, :, k, :] = uf[:, :, k, :] + force[:, k]
                v_new[:, :, k, :] = vs[:, :, k, :] + force[:, 3 + k]

        @pl.when(high)
        def _():
            for k in range(3):
                u_new[:, :, 7 - k, :] = uf[:, :, 7 - k, :] + force[:, k]
                v_new[:, :, 7 - k, :] = vs[:, :, 7 - k, :] + force[:, 3 + k]

        store(u_new, v_new)


def body(displacement, velocity, stiffness, yield_flags, contact, history, kern):
    any_space = pl.BlockSpec(memory_space=pl.ANY)
    dma, vmem = pltpu.SemaphoreType.DMA, pltpu.VMEM
    scratch = [
        vmem((3, OWN + 2, 8, 128), F32),
        vmem((3, OWN + 2, 8, 128), F32),
        vmem((3, OWN + 2, 8, 128), F32),
        vmem((OWN, 8, 128), F32),
        vmem((8, 8, 32), jnp.int32),
        vmem((OWN + 2, 8, 128), F32),
        vmem((OWN, 128), jnp.int32),
        vmem((OWN + 16, 128), F32),
        vmem((N2, 7, 2, 3, 2, 128), BF16),
        vmem((N2, 3, 8, 128), F32),
        vmem((2, 2, 3, N2, 2, 128), F32),
        vmem((128, 256), BF16),
        vmem((192, 256), BF16),
        vmem((256, 192), BF16),
        vmem((128, 256), BF16),
        vmem((2, 64, 128), BF16),
        vmem((2, 64, 128), BF16),
        vmem((32, 128), BF16),
        vmem((4, 128, 128), F32),
        vmem((SUB, 2, 3, OWN, 128), F32),
        vmem((SUB, 2, 3, OWN, 128), F32),
        vmem((NX, YH, NZ, 2, 128), BF16),
        vmem((GROUP, YH, NZ, 2, 128), BF16),
        vmem((NZ, GROUP, YH, 2, 128), BF16),
        vmem((NZ, GROUP, YH, 2, 128), BF16),
        vmem((NZ, GROUP, YH, 2, 128), BF16),
        vmem((NX, NZ, YH, 2, 128), BF16),
        vmem((NZ, GROUP, 2, 128), F32),
        vmem((3, OWN + 16, 128), F32),
        vmem((3, OWN + 16, 128), F32),
        dma((13,)),
        dma((2, N2)),
        dma((4,)),
        dma((SUB, 4)),
        dma((SUB, 4)),
        dma((5,)),
        dma((5,)),
        dma((4, 8)),
        dma((4, 8)),
    ]
    out = jax.ShapeDtypeStruct(displacement.shape, F32)
    in_vmem = pl.BlockSpec(memory_space=pltpu.VMEM)
    fix = lambda x: pltpu.with_memory_space_constraint(x, pltpu.HBM)
    pieces = pl.pallas_call(
        kernel,
        out_shape=(out, out, jax.ShapeDtypeStruct((3, 6, OWN, 128), F32)),
        in_specs=[any_space] * 15,
        out_specs=(in_vmem,) * 3,
        scratch_shapes=scratch,
        compiler_params=pltpu.CompilerParams(
            collective_id=0, has_side_effects=True, vmem_limit_bytes=GRANT
        ),
        name="slab_step",
    )(
        *map(fix, (displacement, velocity, stiffness, yield_flags, contact, history)),
        fix(jnp.swapaxes(kern, 1, 2)), *map(fix, tables()),
    )
    return pl.pallas_call(
        finish,
        out_shape=(out, out),
        in_specs=[in_vmem] * 3,
        out_specs=(any_space, any_space),
        scratch_shapes=[vmem(out.shape, F32), vmem(out.shape, F32), dma((2,))],
        compiler_params=pltpu.CompilerParams(vmem_limit_bytes=GRANT),
        name="slab_finish",
    )(*pieces)


def solution(mesh):
    return jax.shard_map(
        body,
        mesh=mesh,
        in_specs=(
            P(None, "strike", "normal", None),
            P(None, "strike", "normal", None),
            P("strike", "normal", None),
            P("strike", "normal", None),
            P(None, "strike", None),
            P(None, None, None, None, "strike", None),
            P(),
        ),
        out_specs=(P(None, "strike", "normal", None), P(None, "strike", "normal", None)),
        check_vma=False,
    )
```

```python
import functools
import math

import jax
import jax.numpy as jnp
import numpy as np
from jax import lax
from jax.experimental import pallas as pl
from jax.experimental.pallas import tpu as pltpu
from jax.sharding import PartitionSpec as P

MESH = pl.DeviceIdType.MESH
SUB = 3
time_step = 0.5

YH, NZ, NX = 2, 8, 4
GROUP = YH * NX
SLABS = YH * NZ * NX
OWN = 32
WIDE = OWN + 4
NS = SLABS * OWN
N1, N2 = 128, 16
GRANT = 16 * 2**20
F32, BF16 = jnp.float32, jnp.bfloat16


def tables():
    z = np.arange(NZ)[:, None]
    b = np.arange(GROUP)[None, :]
    slab_zb = ((b // NX) * (NZ * NX) + z * NX + b % NX).reshape(-1)
    x4, h2, z8 = np.arange(NX), np.arange(YH), np.arange(NZ)
    slab_xhz = (h2[None, :, None] * (NZ * NX) + z8 * NX + x4[:, None, None]).reshape(-1)
    slab_xzh = (h2 * (NZ * NX) + z8[None, :, None] * NX + x4[:, None, None]).reshape(-1)
    k1 = np.arange(N1)
    n2 = np.arange(N2)
    t = np.arange(N2)
    first = np.concatenate([2 * slab_zb, 2 * slab_zb + 1])
    angle = 2 * np.pi * (np.outer(first, k1) % N1) / N1
    forward = np.concatenate([np.cos(angle), -np.sin(angle)], axis=1)
    twist = 2 * np.pi * np.outer(n2, k1) / NS
    norm = 1.0 / math.sqrt(NS)
    turn = [np.tile(np.cos(twist), (8, 1)), np.tile(-np.sin(twist), (8, 1))]
    small = 2 * np.pi * (np.outer(t, n2) % N2) / N2
    co, si = np.cos(small), np.sin(small)
    inner = np.zeros((2, 3, 2, N2, 2, 2, 4, N2))
    outer = np.zeros((2, 2, 4, N2, 2, 3, 2, N2))
    for c in range(3):
        for dd in range(2):
            inner[0, c, dd, :, 0, dd, c, :] = co
            inner[0, c, dd, :, 1, dd, c, :] = si
            inner[1, c, dd, :, 0, dd, c, :] = -si
            inner[1, c, dd, :, 1, dd, c, :] = co
            outer[0, dd, c, :, 0, c, dd, :] = co.T
            outer[0, dd, c, :, 1, c, dd, :] = -si.T
            outer[1, dd, c, :, 0, c, dd, :] = si.T
            outer[1, dd, c, :, 1, c, dd, :] = co.T
    node = np.concatenate([np.tile(n2, 3), np.zeros(N2, np.int64)])
    for i in range(12):
        c, beyond = (i % 6) // 2, (i % 2) + (16 if i >= 6 else -2)
        node[3 * N2 + i] = beyond
        edge = 2 * np.pi * ((t * beyond) % N2) / N2
        for dd in range(2):
            outer[0, dd, 3, i, 0, c, dd, :] = np.cos(edge)
            outer[0, dd, 3, i, 1, c, dd, :] = -np.sin(edge)
            outer[1, dd, 3, i, 0, c, dd, :] = np.sin(edge)
            outer[1, dd, 3, i, 1, c, dd, :] = np.cos(edge)
    untwist = 2 * np.pi * np.outer(np.tile(node, 2), k1) / NS
    twiddle = norm * np.stack(turn + [np.cos(untwist), np.sin(untwist)])
    inner = inner.reshape(192, 256)
    outer = outer.reshape(256, 192)
    last = np.concatenate([2 * slab_zb, 2 * slab_zb + 1])
    angle = 2 * np.pi * (np.outer(last, k1) % N1) / N1
    inverse = np.concatenate([np.cos(angle), -np.sin(angle)], axis=1)
    dips = np.arange(128)[None, :]
    pack = np.stack([dips == 2 * slab_xhz[:, None] + dd for dd in range(2)])
    unpack = np.stack([dips == 2 * slab_xzh[:, None] + dd for dd in range(2)])
    widen = np.arange(32)[:, None] == dips // 4
    bf = [forward, inner, outer, inverse, pack, unpack, widen]
    return [jnp.asarray(a.astype(np.float32), dtype=BF16) for a in bf] + [
        jnp.asarray(twiddle.astype(np.float32))
    ]


def mm(a, b):
    return jnp.dot(a.astype(BF16), b.astype(BF16), preferred_element_type=F32)


def mm_nt(a, b):
    return lax.dot_general(
        a.astype(BF16), b.astype(BF16), (((1,), (1,)), ((), ())), preferred_element_type=F32
    )


def dip_sides(x):
    axis = x.ndim - 1
    lane = lax.broadcasted_iota(jnp.int32, x.shape, axis)
    below = jnp.where(lane == 0, 0.0, pltpu.roll(x, 1, axis))
    above = jnp.where(lane == 127, 0.0, pltpu.roll(x, 127, axis))
    return below + above


def kernel(
    u_in, v_in, stiff_in, flags_in, contact_in, history_in, kern_in,
    forward_in, inner_in, outer_in, inverse_in, pack_in, unpack_in, widen_in, twiddle_in,
    uf, vs,
    us0, us1, us2, vx, vy, stiff, flags, mods, marked, contacts, history, kern, past,
    forward, inner, outer, inverse, pack, unpack, widen, twiddle,
    faces, sides, p1, g1, r1, p2, g2, q2, wide, spread, pulls, mod2,
    in_sem, past_sem, self_sem, halo_s, halo_r, aux_s, aux_r, a2a_s, a2a_r,
):
    s = lax.axis_index("strike")
    m = lax.axis_index("normal")
    my_z = (s // NX) % NZ
    my_b = (s // (NX * NZ)) * NX + s % NX
    low, high = m == 0, m == 7
    plane = jnp.logical_or(low, high)
    face = m // 7
    left, right = (s + SLABS - 1) % SLABS, (s + 1) % SLABS
    mine_b_base = (my_b // NX) * (NZ * NX) + my_b % NX
    my_x = s % NX
    early = my_b < NX
    owner = jnp.logical_and(plane, early)
    feeder = jnp.logical_and(plane, jnp.logical_not(early))

    def x_peer(i):
        x = (my_x + i) % NX
        return x, my_z * NX + x

    def z_peer(i):
        z = (my_z + i) % NZ
        return z, mine_b_base + z * NX

    def b_peer(i):
        b = (my_b + i) % GROUP
        return b, (b // NX) * (NZ * NX) + my_z * NX + b % NX

    barrier = pltpu.get_barrier_semaphore()

    def greet(**where):
        pl.semaphore_signal(barrier, inc=1, device_id=where, device_id_type=MESH)

    greet(strike=left)
    greet(strike=right)

    @pl.when(jnp.logical_not(low))
    def _():
        greet(normal=m - 1)

    @pl.when(jnp.logical_not(high))
    def _():
        greet(normal=m + 1)

    @pl.when(owner)
    def _():
        for i in range(1, NZ):
            greet(strike=z_peer(i)[1])
        for i in range(1, GROUP):
            greet(strike=b_peer(i)[1])

    @pl.when(feeder)
    def _():
        for i in range(NX):
            greet(strike=x_peer(i)[1])

    loads = [
        pltpu.make_async_copy(u_in, us0.at[:, pl.ds(3, OWN)], in_sem.at[0]),
        pltpu.make_async_copy(pack_in, pack, in_sem.at[1]),
        pltpu.make_async_copy(flags_in, flags, in_sem.at[2]),
        pltpu.make_async_copy(stiff_in, stiff, in_sem.at[3]),
        pltpu.make_async_copy(widen_in, widen, in_sem.at[4]),
        pltpu.make_async_copy(contact_in.at[face], marked, in_sem.at[5]),
        pltpu.make_async_copy(v_in, vx.at[:, pl.ds(2, OWN)], in_sem.at[6]),
        pltpu.make_async_copy(forward_in, forward, in_sem.at[7]),
        pltpu.make_async_copy(inner_in, inner, in_sem.at[8]),
        pltpu.make_async_copy(outer_in, outer, in_sem.at[9]),
        pltpu.make_async_copy(inverse_in, inverse, in_sem.at[10]),
        pltpu.make_async_copy(unpack_in, unpack, in_sem.at[11]),
        pltpu.make_async_copy(twiddle_in, twiddle, in_sem.at[12]),
    ]
    for load in loads:
        load.start()
    past_loads = []
    for t in range(N2):
        lanes = pl.ds(128 * t, 128)
        past_loads += [
            pltpu.make_async_copy(
                history_in.at[face, pl.ds(0, 7), :, :, :, lanes], history.at[t], past_sem.at[0, t]
            ),
            pltpu.make_async_copy(kern_in.at[face, :, :, lanes], kern.at[t], past_sem.at[1, t]),
        ]

    def strike_copies():
        copies = []
        for k, (ref, depth) in enumerate(((us0, 3), (vx, 2), (mods, 2))):
            def part(start, ref=ref, depth=depth):
                window = pl.ds(start, depth)
                return ref.at[window] if ref is mods else ref.at[:, window]

            copies += [
                pltpu.make_async_remote_copy(
                    part(OWN), part(0), aux_s.at[2 * k], aux_r.at[2 * k],
                    device_id={"strike": right}, device_id_type=MESH,
                ),
                pltpu.make_async_remote_copy(
                    part(depth), part(OWN + depth), aux_s.at[2 * k + 1], aux_r.at[2 * k + 1],
                    device_id={"strike": left}, device_id_type=MESH,
                ),
            ]
        return copies

    def up_copy(i):
        return pltpu.make_async_remote_copy(
            faces.at[i, 1], sides.at[i, 0], halo_s.at[i, 0], halo_r.at[i, 0],
            device_id={"normal": m + 1}, device_id_type=MESH,
        )

    def down_copy(i):
        return pltpu.make_async_remote_copy(
            faces.at[i, 0], sides.at[i, 1], halo_s.at[i, 1], halo_r.at[i, 1],
            device_id={"normal": m - 1}, device_id_type=MESH,
        )

    def start_halo(i):
        @pl.when(jnp.logical_not(high))
        def _():
            up_copy(i).start()

        @pl.when(jnp.logical_not(low))
        def _():
            down_copy(i).start()

    def wait_halo(i):
        @pl.when(jnp.logical_not(low))
        def _():
            up_copy(i).wait_recv()

        @pl.when(jnp.logical_not(high))
        def _():
            down_copy(i).wait_recv()

    def finish_halo(i):
        @pl.when(jnp.logical_not(high))
        def _():
            up_copy(i).wait_send()

        @pl.when(jnp.logical_not(low))
        def _():
            down_copy(i).wait_send()

    def set_faces(i, src, first):
        faces[i, 0] = src[:, first : first + WIDE, 0, :]
        faces[i, 1] = src[:, first : first + WIDE, 7, :]

    marks_around = [
        pltpu.make_async_remote_copy(
            contacts.at[pl.ds(OWN, 8)], contacts.at[pl.ds(0, 8)], aux_s.at[6], aux_r.at[6],
            device_id={"strike": right}, device_id_type=MESH,
        ),
        pltpu.make_async_remote_copy(
            contacts.at[pl.ds(8, 8)], contacts.at[pl.ds(OWN + 8, 8)], aux_s.at[7], aux_r.at[7],
            device_id={"strike": left}, device_id_type=MESH,
        ),
    ]

    def send(k, i, j, src, dst, who):
        return pltpu.make_async_remote_copy(
            src, dst, a2a_s.at[k, i], a2a_r.at[k, j],
            device_id={"strike": who}, device_id_type=MESH,
        )

    def gather_sends(first):
        return [
            send(0, i, my_b, p1.at[x_peer(i)[0]], g1.at[my_b], x_peer(i)[1])
            for i in range(first, NX)
        ]

    def gather_self():
        return pltpu.make_async_copy(p1.at[my_x], g1.at[my_b], self_sem.at[0])

    def gather_lands():
        return [
            send(0, 0, b_peer(i)[0], p1.at[0], g1.at[b_peer(i)[0]], s ^ 1)
            for i in range(1, GROUP)
        ]

    def turn_sends():
        return [
            send(1, i, i, g1.at[:, :, z_peer(i)[0]], r1.at[my_z], z_peer(i)[1])
            for i in range(1, NZ)
        ]

    def turn_self():
        return pltpu.make_async_copy(g1.at[:, :, my_z], r1.at[my_z], self_sem.at[1])

    def return_sends():
        return [
            send(2, i, i, p2.at[z_peer(i)[0]], g2.at[my_z], z_peer(i)[1]) for i in range(1, NZ)
        ]

    def return_self():
        return pltpu.make_async_copy(p2.at[my_z], g2.at[my_z], self_sem.at[2])

    def scatter_sends():
        return [
            send(3, i, my_x, g2.at[:, b_peer(i)[0]], q2.at[my_x], b_peer(i)[1])
            for i in range(1, GROUP)
        ]

    def scatter_self():
        return pltpu.make_async_copy(g2.at[:, my_b], q2.at[my_x], self_sem.at[3])

    def scatter_lands(first):
        return [
            send(3, 0, x_peer(i)[0], g2.at[:, 0], q2.at[x_peer(i)[0]], s ^ 1)
            for i in range(first, NX)
        ]

    def past_copy(who):
        return pltpu.make_async_remote_copy(
            past.at[0], past.at[1], aux_s.at[8], aux_r.at[8],
            device_id={"strike": who}, device_id_type=MESH,
        )

    def start_all(copies):
        for copy in copies:
            copy.start()

    def recv_all(copies):
        for copy in copies:
            copy.wait_recv()

    def sent_all(copies):
        for copy in copies:
            copy.wait_send()

    loads[0].wait()
    loads[1].wait()

    @pl.when(plane)
    def _():
        for jh in range(2):
            rows = []
            for c in range(3):
                a = 3 + 16 * jh
                rows.append(jnp.where(high, us0[c, a : a + 16, 7, :], us0[c, a : a + 16, 0, :]))
            rows.append(jnp.zeros((16, 128), F32))
            block = jnp.concatenate(rows, axis=0)
            halves = [mm_nt(pack[dd], block) for dd in range(2)]
            wide[:, :, jh, :] = jnp.concatenate(halves, axis=1).reshape(NZ, GROUP, 128)
        p1[...] = wide[...].reshape(NX, YH, NZ, 2, 128).astype(BF16)

    def prepare():
        loads[2].wait()
        loads[3].wait()
        loads[4].wait()
        marks = mm(flags[...].reshape(64, 32).astype(F32), widen[...]).reshape(8, 1, 8, 128)
        scale = 1.0 - 0.5 * marks
        mods[2 : OWN + 2] = (stiff[...].reshape(8, 4, 8, 128) * scale).reshape(OWN, 8, 128)
        loads[5].wait()
        contacts[8 : OWN + 8] = marked[...].astype(F32)
        loads[6].wait()

    @pl.when(feeder)
    def _():
        pl.semaphore_wait(barrier, 3 + NX)
        start_all(gather_sends(0))

    @pl.when(plane)
    def _():
        start_all(past_loads)

    @pl.when(low)
    def _():
        for i in range(SUB):
            sides[i, 0] = jnp.zeros((3, WIDE, 128), F32)

    @pl.when(high)
    def _():
        for i in range(SUB):
            sides[i, 1] = jnp.zeros((3, WIDE, 128), F32)

    us2[:, 0] = jnp.zeros((3, 8, 128), F32)
    us2[:, WIDE - 1] = jnp.zeros((3, 8, 128), F32)
    prepare()

    @pl.when(owner)
    def _():
        pl.semaphore_wait(barrier, 3 + NZ - 1 + GROUP - 1)
        start_all(gather_sends(1))
        gather_self().start()

    @pl.when(jnp.logical_not(plane))
    def _():
        pl.semaphore_wait(barrier, 4)

    start_all(strike_copies())
    start_all(marks_around)

    @pl.when(plane)
    def _():
        for load in past_loads:
            load.wait()
        for c in range(3):
            for q in range(2):
                total = jnp.zeros((N2, 2, 128), F32)
                for lag in range(7):
                    weight = kern[:, c, lag + 1, :][:, None, :]
                    total = total + weight * history[:, lag, q, c].astype(F32)
                past[0, q, c] = total

    @pl.when(feeder)
    def _():
        past_copy(s - NZ * NX).start()

    def substep(i, src, base, dst, first, count):
        for c in range(3):
            a, b = first + base, first + count + base
            here = src[c, a:b]
            layer = lax.broadcasted_iota(jnp.int32, here.shape, 1)
            under = sides[i, 0, c, first : first + count]
            over = sides[i, 1, c, first : first + count]
            below = jnp.where(layer == 0, under[:, None, :], pltpu.roll(here, 1, 1))
            above = jnp.where(layer == 7, over[:, None, :], pltpu.roll(here, 7, 1))
            lap = (
                src[c, a + 1 : b + 1] + src[c, a - 1 : b - 1]
                + (above + below) + dip_sides(here) - 6.0 * here
            )
            rows = slice(first, first + count)
            speed = (vx if i == 0 else vy)[c, rows] + time_step * (mods[rows] * lap)
            moved = here + time_step * speed
            if dst is uf:
                vs[c] = speed
                uf[c] = moved
            else:
                vy[c, rows] = speed
                dst[c, rows] = moved

    @pl.when(owner)
    def _():
        recv_all(gather_lands())
        gather_self().wait()
        start_all(turn_sends())
        turn_self().start()

    recv_all(strike_copies())
    set_faces(0, us0, 1)
    start_halo(0)
    for load in loads[7:]:
        load.wait()
    wait_halo(0)
    substep(0, us0, 1, us1, 0, WIDE)
    set_faces(1, us1, 0)
    start_halo(1)

    @pl.when(owner)
    def _():
        newest = jnp.concatenate([kern[:, c, 0, :] for c in range(3) for _ in range(2)], axis=0)
        newest = jnp.concatenate([newest, newest], axis=0)
        recv_all(turn_sends())
        turn_self().wait()
        past_copy(s ^ 1).wait_recv()
        pairs = range(YH)
        spread[...] = r1[...].astype(F32)
        got = jnp.concatenate(
            [
                jnp.concatenate(
                    [spread[:, :, h, jh, :].reshape(SLABS, 128) for jh in range(2)], axis=0
                )
                for h in pairs
            ],
            axis=1,
        )
        y = mm(got.T, forward[...])
        tr, ti = twiddle[0], twiddle[1]
        turned = []
        for h in pairs:
            re, im = y[128 * h : 128 * h + 128, :128], y[128 * h : 128 * h + 128, 128:]
            turned.append(jnp.concatenate([re * tr - im * ti, re * ti + im * tr], axis=0))
        modes = mm(inner[...], jnp.concatenate(turned, axis=1))
        forces = []
        for h in pairs:
            older = jnp.concatenate(
                [past[h, q, c, :, dd, :] for q in range(2) for c in range(3) for dd in range(2)],
                axis=0,
            )
            forces.append(newest * modes[:, 128 * h : 128 * h + 128] + older)
        back = mm(outer[...], jnp.concatenate(forces, axis=1))
        tr, ti = twiddle[2], twiddle[3]
        turned = []
        for h in pairs:
            re, im = back[:128, 128 * h : 128 * h + 128], back[128:, 128 * h : 128 * h + 128]
            turned.append(jnp.concatenate([re * tr - im * ti, re * ti + im * tr], axis=1))
        pulled = mm_nt(inverse[...], jnp.concatenate(turned, axis=0))
        for h in pairs:
            for jh in range(2):
                block = pulled[64 * jh : 64 * jh + 64, 128 * h : 128 * h + 128]
                spread[:, :, h, jh, :] = block.reshape(NZ, GROUP, 128)
        p2[...] = spread[...].astype(BF16)
        start_all(return_sends())
        return_self().start()

    wait_halo(1)
    substep(1, us1, 0, us2, 1, WIDE - 2)
    set_faces(2, us2, 0)
    start_halo(2)

    @pl.when(owner)
    def _():
        recv_all(return_sends())
        return_self().wait()
        start_all(scatter_sends())
        scatter_self().start()

    wait_halo(2)
    substep(2, us2, 0, uf, 2, OWN)
    recv_all(marks_around)

    @pl.when(plane)
    def _():
        mod2[...] = jnp.zeros_like(mod2)
        pulls[...] = jnp.zeros_like(pulls)
        for k in range(3):
            mod2[k, 7:41] = jnp.where(
                high, mods[1 : OWN + 3, 7 - k, :], mods[1 : OWN + 3, k, :]
            )

    @pl.when(owner)
    def _():
        recv_all(scatter_lands(1))
        scatter_self().wait()

    @pl.when(feeder)
    def _():
        recv_all(scatter_lands(0))

    @pl.when(plane)
    def _():
        wide[...] = q2[...].astype(F32).reshape(NZ, GROUP, 2, 128)
        turned = jnp.concatenate(
            [wide[:, :, jh, :].reshape(SLABS, 128) for jh in range(2)], axis=1
        ).T
        pieces = sum(
            mm(
                jnp.concatenate(
                    [turned[64 * dd : 64 * dd + 64], turned[128 + 64 * dd : 192 + 64 * dd]], axis=0
                ),
                unpack[dd],
            )
            for dd in range(2)
        )
        pieces = [pieces[:64], pieces[64:]]

        def lap2(x):
            return pltpu.roll(x, 1, 0) + pltpu.roll(x, 47, 0) + dip_sides(x) - 6.0 * x

        half = time_step
        responses = []
        for c in range(3):
            a = 16 * c
            pulls[c, 6:8] = pieces[0][48 + 2 * c : 50 + 2 * c]
            pulls[c, 8:24] = pieces[0][a : a + 16]
            pulls[c, 24:40] = pieces[1][a : a + 16]
            pulls[c, 40:42] = pieces[1][54 + 2 * c : 56 + 2 * c]
            load = contacts[...] * pulls[c]
            v0 = half * load
            u0 = half * v0
            v0, v1 = v0 + half * (mod2[0] * lap2(u0) + load), half * (mod2[1] * u0)
            u0, u1 = u0 + half * v0, half * v1
            v0, v1, v2 = (
                v0 + half * (mod2[0] * (lap2(u0) + u1) + load),
                v1 + half * (mod2[1] * (lap2(u1) + u0)),
                half * (mod2[2] * u1),
            )
            u0, u1, u2 = u0 + half * v0, u1 + half * v1, half * v2
            responses.append([x[8:40] for x in (u0, u1, u2, v0, v1, v2)])

        @pl.when(low)
        def _():
            for c in range(3):
                for k in range(3):
                    uf[c, :, k, :] = uf[c, :, k, :] + responses[c][k]
                    vs[c, :, k, :] = vs[c, :, k, :] + responses[c][3 + k]

        @pl.when(high)
        def _():
            for c in range(3):
                for k in range(3):
                    uf[c, :, 7 - k, :] = uf[c, :, 7 - k, :] + responses[c][k]
                    vs[c, :, 7 - k, :] = vs[c, :, 7 - k, :] + responses[c][3 + k]

    for i in range(SUB):
        finish_halo(i)
    sent_all(strike_copies() + marks_around)

    @pl.when(owner)
    def _():
        sent_all(gather_sends(1) + turn_sends() + return_sends() + scatter_sends())

    @pl.when(feeder)
    def _():
        sent_all(gather_sends(0))
        past_copy(s - NZ * NX).wait_send()


def finish(uf, vs, u_out, v_out, sem):
    copies = [
        pltpu.make_async_copy(uf, u_out, sem.at[0]),
        pltpu.make_async_copy(vs, v_out, sem.at[1]),
    ]
    for copy in copies:
        copy.start()
    for copy in copies:
        copy.wait()


def body(displacement, velocity, stiffness, yield_flags, contact, history, kern):
    any_space = pl.BlockSpec(memory_space=pl.ANY)
    dma, vmem = pltpu.SemaphoreType.DMA, pltpu.VMEM
    scratch = [
        vmem((3, OWN + 6, 8, 128), F32),
        vmem((3, WIDE, 8, 128), F32),
        vmem((3, WIDE, 8, 128), F32),
        vmem((3, WIDE, 8, 128), F32),
        vmem((3, WIDE, 8, 128), F32),
        vmem((OWN, 8, 128), F32),
        vmem((8, 8, 32), jnp.int32),
        vmem((WIDE, 8, 128), F32),
        vmem((OWN, 128), jnp.int32),
        vmem((OWN + 16, 128), F32),
        vmem((N2, 7, 2, 3, 2, 128), BF16),
        vmem((N2, 3, 8, 128), F32),
        vmem((2, 2, 3, N2, 2, 128), F32),
        vmem((128, 256), BF16),
        vmem((192, 256), BF16),
        vmem((256, 192), BF16),
        vmem((128, 256), BF16),
        vmem((2, 64, 128), BF16),
        vmem((2, 64, 128), BF16),
        vmem((32, 128), BF16),
        vmem((4, 128, 128), F32),
        vmem((SUB, 2, 3, WIDE, 128), F32),
        vmem((SUB, 2, 3, WIDE, 128), F32),
        vmem((NX, YH, NZ, 2, 128), BF16),
        vmem((GROUP, YH, NZ, 2, 128), BF16),
        vmem((NZ, GROUP, YH, 2, 128), BF16),
        vmem((NZ, GROUP, YH, 2, 128), BF16),
        vmem((NZ, GROUP, YH, 2, 128), BF16),
        vmem((NX, NZ, YH, 2, 128), BF16),
        vmem((NZ, GROUP, 2, 128), F32),
        vmem((NZ, GROUP, YH, 2, 128), F32),
        vmem((3, OWN + 16, 128), F32),
        vmem((3, OWN + 16, 128), F32),
        dma((13,)),
        dma((2, N2)),
        dma((4,)),
        dma((SUB, 2)),
        dma((SUB, 2)),
        dma((9,)),
        dma((9,)),
        dma((4, 8)),
        dma((4, 8)),
    ]
    out = jax.ShapeDtypeStruct(displacement.shape, F32)
    in_vmem = pl.BlockSpec(memory_space=pltpu.VMEM)
    fix = lambda x: pltpu.with_memory_space_constraint(x, pltpu.HBM)
    pieces = pl.pallas_call(
        kernel,
        out_shape=(out, out),
        in_specs=[any_space] * 15,
        out_specs=(in_vmem,) * 2,
        scratch_shapes=scratch,
        compiler_params=pltpu.CompilerParams(
            collective_id=0, has_side_effects=True, vmem_limit_bytes=GRANT
        ),
        name="slab_step",
    )(
        *map(fix, (displacement, velocity, stiffness, yield_flags, contact, history)),
        fix(jnp.swapaxes(kern, 1, 2)), *map(fix, tables()),
    )
    return pl.pallas_call(
        finish,
        out_shape=(out, out),
        in_specs=[in_vmem] * 2,
        out_specs=(any_space, any_space),
        scratch_shapes=[dma((2,))],
        compiler_params=pltpu.CompilerParams(vmem_limit_bytes=GRANT),
        name="slab_finish",
    )(*pieces)


def solution(mesh):
    return jax.shard_map(
        body,
        mesh=mesh,
        in_specs=(
            P(None, "strike", "normal", None),
            P(None, "strike", "normal", None),
            P("strike", "normal", None),
            P("strike", "normal", None),
            P(None, "strike", None),
            P(None, None, None, None, "strike", None),
            P(),
        ),
        out_specs=(P(None, "strike", "normal", None), P(None, "strike", "normal", None)),
        check_vma=False,
    )
```
